512 devices in a mesh: row: 16 (over y, core), col: 32 (over x, z).
Axes of the slice: x: 4, y: 8, z: 8, core: 2. Of those that a mesh axis runs over, the one named last changes fastest.
Arguments:
- features: bfloat16 [65536, 128], P('col', 'row'), may hold values from -6 to 6
- weight: bfloat16 [128, 128], replicated, may hold values from -0.5 to 0.5
- bias_vector: float32 [128], replicated, may hold values from -3 to 3
- tile_rows: int32 [16, 32, 128], P('row', 'col'), may hold values from 0 to 31
- tile_cols: int32 [16, 32, 128], P('row', 'col'), may hold values from 0 to 15
- neighbours: int32 [16, 32, 128, 2, 128], P('row', 'col'), may hold values from 0 to 127, as said below
- edge_weights: bfloat16 [16, 32, 128, 2, 128], P('row', 'col'), may hold values from 0.039794922 to 0.3984375
- tile_count: int32 [16, 32], P('row', 'col'), may hold values from 16 to 128, as said below
- cotangent: float32 [65536, 128], P(('row', 'col')), may hold values from -6 to 6
Outputs:
- activations: float32 [65536, 128], P(('row', 'col'))
- grad_features: bfloat16 [65536, 128], P('col', 'row')
- grad_weight: float32 [128, 128], replicated
- grad_bias: float32 [128], replicated
The draws below stay inside these ranges and needn't reach their ends.
Inputs may be any that keep to these rules, and one draw needn't show every extreme that they name: `tile_count`: one device uses all 128 tile slots in every draw. The 2 neighbours of one galaxy within one tile are distinct.
All inputs are finite; a program needn't handle non-finite values.
Results may differ from the reference program's by a relative error of at most 0.006.
Values may be sent and summed in bfloat16 or wider, within the bound.
A program may use at most 64 MiB of HBM per device.

```python
import math
import jax
import jax.numpy as jnp
from jax import lax

HID = 128
TILE = 128
NBR = 2
TILE_MAX = 128
ROW_BLOCKS = 32
COL_BLOCKS = 16
NODES = 65536
N_ROW = 16
N_COL = 32


def draw_neighbours(key, part):
    window_span = TILE // NBR
    full_shape = (N_ROW, N_COL, TILE_MAX, NBR, TILE)
    offsets = jax.random.randint(jax.random.fold_in(key, 11), full_shape, 0, window_span)
    rotation = jax.random.randint(jax.random.fold_in(key, 12), (N_ROW, N_COL, TILE_MAX, 1, TILE), 0, TILE)
    lane_start = jnp.arange(NBR, dtype=jnp.int32).reshape(1, 1, 1, NBR, 1) * window_span
    return ((offsets + lane_start + rotation) % TILE).astype(jnp.int32)


def draw_tile_count(key, part):
    counts = jax.random.randint(jax.random.fold_in(key, 21), (N_ROW * N_COL,), TILE_MAX // 8, 3 * TILE_MAX // 8 + 1)
    chosen = jax.random.randint(jax.random.fold_in(key, 22), (), 0, N_ROW * N_COL)
    device_ids = jnp.arange(N_ROW * N_COL, dtype=jnp.int32)
    counts = jnp.where(device_ids == chosen, TILE_MAX, counts)
    return counts.reshape(N_ROW, N_COL).astype(jnp.int32)


def with_ends(values, own_key, least, top_value):
    index_at = [jax.random.randint(jax.random.fold_in(own_key, axis), (), 0, length) for axis, length in enumerate(values.shape)]
    main_axis = values.shape.index(max(values.shape))
    beside = index_at[:main_axis] + [(index_at[main_axis] + 1) % values.shape[main_axis]] + index_at[main_axis + 1:]
    return values.at[tuple(index_at)].set(least).at[tuple(beside)].set(top_value)


def level_of(own_key, dims, cuts, smallest, high):
    gain = 1.0
    for position, shards_of in cuts:
        draws = jax.random.uniform(jax.random.fold_in(jax.random.fold_in(own_key, 6), position), (shards_of,), jnp.float32, smallest / len(cuts), high / len(cuts))
        gain = gain * jnp.repeat(jnp.exp(draws), dims[position] // shards_of).reshape((-1,) + (1,) * (len(dims) - 1 - position))
    return gain


def normal_values(own_key, extent, width, limit, shards=(), kind=jnp.bfloat16):
    entries = jax.random.normal(own_key, extent, jnp.float32) * width
    if len(shards) > 0:
        entries = level_of(own_key, extent, shards, -0.22, 0.18) * entries
    return jnp.clip(entries, min=-limit, max=limit).astype(kind)


def setup_inputs(seed: int = 0) -> dict:
    arg_keys = jax.random.split(jax.random.key(seed), 10)
    features = normal_values(arg_keys[0], (NODES, HID), 1.0, 6.0, ((0, 32), (1, 16)))
    weight = normal_values(arg_keys[1], (HID, HID), HID ** -0.5, 0.5)
    bias_vector = normal_values(arg_keys[2], (HID,), 0.5, 3.0, (), jnp.float32)
    tile_rows = with_ends(jax.random.randint(arg_keys[3], (N_ROW, N_COL, TILE_MAX), 0, ROW_BLOCKS), jax.random.fold_in(arg_keys[3], 1), 0, ROW_BLOCKS - 1).astype(jnp.int32)
    tile_cols = with_ends(jax.random.randint(arg_keys[4], (N_ROW, N_COL, TILE_MAX), 0, COL_BLOCKS), jax.random.fold_in(arg_keys[4], 1), 0, COL_BLOCKS - 1).astype(jnp.int32)
    neighbours = draw_neighbours(jax.random.fold_in(arg_keys[9], 71), 0)
    edge_weights = jnp.clip(jnp.exp(math.log(0.3984375) - 2.3038113 * jax.random.uniform(arg_keys[6], (N_ROW, N_COL, TILE_MAX, NBR, TILE), jnp.float32) ** level_of(arg_keys[6], (N_ROW, N_COL, TILE_MAX, NBR, TILE), ((0, 16), (1, 32)), -0.2, 0.2)), 0.039794922, 0.3984375).astype(jnp.bfloat16)
    tile_count = draw_tile_count(jax.random.fold_in(arg_keys[9], 71), 0)
    cotangent = normal_values(arg_keys[8], (NODES, HID), 1.0, 6.0, ((0, 512),), jnp.float32)
    return dict(features=features, weight=weight, bias_vector=bias_vector, tile_rows=tile_rows, tile_cols=tile_cols, neighbours=neighbours, edge_weights=edge_weights, tile_count=tile_count, cotangent=cotangent)


def edge_lists(tile_rows, tile_cols, neighbours, edge_weights, tile_count, node_count):
    row_nodes = node_count // N_ROW
    col_nodes = node_count // N_COL
    slot_ids = jnp.arange(TILE_MAX, dtype=jnp.int32).reshape(1, 1, TILE_MAX)
    live_slot = slot_ids < tile_count[:, :, None]
    row_owner = jnp.arange(N_ROW, dtype=jnp.int32).reshape(N_ROW, 1, 1) * row_nodes
    col_owner = jnp.arange(N_COL, dtype=jnp.int32).reshape(1, N_COL, 1) * col_nodes
    row_first = row_owner + tile_rows * TILE
    col_first = col_owner + tile_cols * TILE
    galaxy = jnp.arange(TILE, dtype=jnp.int32).reshape(1, 1, 1, 1, TILE)
    targets = row_first[:, :, :, None, None] + galaxy + jnp.zeros_like(neighbours)
    sources = col_first[:, :, :, None, None] + neighbours
    values = jnp.where(live_slot[:, :, :, None, None], edge_weights.astype(jnp.float32), jnp.zeros((), jnp.float32))
    pairs_total = N_ROW * N_COL
    return targets.reshape(pairs_total, -1), sources.reshape(pairs_total, -1), values.reshape(pairs_total, -1)


def spread(source_rows, targets, sources, values, node_count):
    def accumulate(summed, edge_block):
        target, source, weight_row = edge_block
        summed = summed.at[target].add(weight_row[:, None] * source_rows[source].astype(jnp.float32))
        return summed, None

    zeroes = jnp.zeros((node_count, source_rows.shape[1]), jnp.float32)
    summed, _ = lax.scan(accumulate, zeroes, (targets, sources, values))
    return summed


def reference(features, weight, bias_vector, tile_rows, tile_cols, neighbours, edge_weights, tile_count, cotangent):
    node_count = features.shape[0]
    targets, sources, values = edge_lists(tile_rows, tile_cols, neighbours, edge_weights, tile_count, node_count)
    projected = jnp.dot(features, weight, preferred_element_type=jnp.float32).astype(jnp.bfloat16)
    pre = spread(projected, targets, sources, values, node_count) + bias_vector
    squashed = jax.nn.sigmoid(pre)
    activations = pre * squashed
    pre_grad = (cotangent * squashed * (1.0 + pre * (1.0 - squashed))).astype(jnp.bfloat16)
    proj_grad = spread(pre_grad, sources, targets, values, node_count)
    shrink = float(node_count) ** -0.5
    weight_wide = weight.astype(jnp.float32)
    grad_features = jnp.dot(proj_grad, weight_wide.T, precision=lax.Precision.HIGHEST).astype(jnp.bfloat16)
    grad_weight = jnp.dot(features.astype(jnp.float32).T, proj_grad, precision=lax.Precision.HIGHEST) * shrink
    grad_bias = jnp.sum(pre_grad.astype(jnp.float32), axis=0) * shrink
    return activations, grad_features, grad_weight, grad_bias
```

```python
import functools

import jax
import jax.numpy as jnp
from jax import lax
from jax.experimental import pallas as pl
from jax.experimental.pallas import tpu as pltpu
from jax.sharding import PartitionSpec as P

NX = 4
NZ = 8
NY = 8
NK = 2
T = 128
F32 = jnp.float32
BF16 = jnp.bfloat16
MESH = pl.DeviceIdType.MESH
VMEM_SPEC = pl.BlockSpec(memory_space=pltpu.VMEM)
SMEM_SPEC = pl.BlockSpec(memory_space=pltpu.SMEM)
HALF_A = (4, 3, 2, 1)
HALF_B = (5, 6, 7, 0)


def place():
    row = lax.axis_index("row")
    col = lax.axis_index("col")
    return row, col, row // NK, row % NK, col // NZ, col % NZ


def meet(peers):
    barrier = pltpu.get_barrier_semaphore()
    for peer in peers:
        pl.semaphore_signal(barrier, inc=1, device_id=peer, device_id_type=MESH)
    pl.semaphore_wait(barrier, len(peers))


def remote(src, dst, send_sem, recv_sem, peer):
    return pltpu.make_async_remote_copy(
        src_ref=src,
        dst_ref=dst,
        send_sem=send_sem,
        recv_sem=recv_sem,
        device_id=peer,
        device_id_type=MESH,
    )


def gather_kernel(ft_ref, out_ref, ysend, yrecv, psend, precv):
    row, col, y, k, x, z = place()
    partner = (y * NK + 1 - k, col)
    ypeer = lambda d: (lax.rem(y + d, NY) * NK + k, col)
    meet([partner] + [ypeer(d) for d in range(1, NY)])
    order = (4, 3, 5, 2, 6, 1, 7)
    started = []
    for d in order:
        copy = remote(ft_ref, out_ref.at[row], ysend.at[d], yrecv.at[d], ypeer(d))
        copy.start()
        started.append(copy)
    mine = remote(ft_ref, out_ref.at[row], psend.at[0], precv.at[0], partner)
    mine.start()
    started.append(mine)
    out_ref[row] = ft_ref[...]
    for d in (1, 7, 2, 6, 3, 5, 4):
        slot = lax.rem(y + NY - d, NY) * NK + k
        remote(ft_ref, out_ref.at[slot], ysend.at[d], yrecv.at[d], ypeer(d)).wait_recv()
        copy = remote(out_ref.at[slot], out_ref.at[slot], psend.at[d], precv.at[d], partner)
        copy.start()
        started.append(copy)
    for d in range(NY):
        slot = lax.rem(y + NY - d, NY) * NK + 1 - k
        remote(ft_ref, out_ref.at[slot], psend.at[d], precv.at[d], partner).wait_recv()
    for copy in started:
        copy.wait_send()


def tile_matrix(t, live, nb_ref, ew_ref, rows_iota):
    ids = nb_ref[t]
    values = ew_ref[t].astype(F32)
    values = jnp.where(live, values, jnp.zeros_like(values))
    second = jnp.where(rows_iota == ids[1:2, :], values[1:2, :], 0.0)
    return jnp.where(rows_iota == ids[0:1, :], values[0:1, :], second).astype(BF16)


def forward_kernel(unroll, rows_ref, cols_ref, count_ref, ft_ref, nb_ref, ew_ref, out_ref, acc):
    acc[...] = jnp.zeros_like(acc)
    count = count_ref[0]
    iota = lax.broadcasted_iota(jnp.int32, (T, T), 0)

    def body(g, carry):
        for u in range(unroll):
            t = g * unroll + u
            dense = tile_matrix(t, t < count, nb_ref, ew_ref, iota)
            c = pl.multiple_of(cols_ref[t] * T, T)
            prod = jnp.dot(ft_ref[:, pl.ds(c, T)], dense, preferred_element_type=F32)
            r = rows_ref[t]
            acc[r] += prod
        return carry

    lax.fori_loop(0, (count + unroll - 1) // unroll, body, 0)
    out_ref[...] = acc[...].astype(BF16)


def backward_kernel(unroll, rows_ref, cols_ref, count_ref, g_ref, w_ref, nb_ref, ew_ref, out_ref, acc):
    acc[...] = jnp.zeros_like(acc)
    count = count_ref[0]
    iota = lax.broadcasted_iota(jnp.int32, (T, T), 0)

    def body(g, carry):
        for u in range(unroll):
            t = g * unroll + u
            dense = tile_matrix(t, t < count, nb_ref, ew_ref, iota)
            prod = jnp.dot(dense, g_ref[rows_ref[t]], preferred_element_type=F32)
            c = cols_ref[t]
            acc[c] += prod
        return carry

    lax.fori_loop(0, (count + unroll - 1) // unroll, body, 0)
    contract = (((1,), (1,)), ((), ()))
    for c in range(acc.shape[0]):
        high = acc[c].astype(BF16)
        low = (acc[c] - high.astype(F32)).astype(BF16)
        term = lax.dot_general(w_ref[...], high, contract, preferred_element_type=F32)
        term += lax.dot_general(w_ref[...], low, contract, preferred_element_type=F32)
        out_ref[:, c * T : (c + 1) * T] = term.astype(BF16)


def middle_kernel(
    u_ref, w_ref, bias_ref, cot_ref,
    act_ref, band_ref, wsum_ref,
    from_l_relay, from_r_relay, to_r, to_l, in_l, in_r, summed, zin, own, wbuf, wxin, wz, wzin,
    s_raw_r, s_raw_l, s_mix_r, s_mix_l, r_relay_l, r_relay_r, r_in_l, r_in_r,
    s_z, r_z, s_gz, r_gz, s_gr, s_gl, r_gl, r_gr, s_rel, r_rel, s_wx, r_wx, s_wz, r_wz,
):
    row, col, y, k, x, z = place()
    right = lax.rem(x + 1, NX)
    left = lax.rem(x + NX - 1, NX)
    across = lax.rem(x + 2, NX)
    xdev = lambda xx: (row, xx * NZ + z)
    zof = lambda d: lax.rem(z + d, NZ)
    zfrom = lambda d: lax.rem(z + NZ - d, NZ)
    zdev = lambda d: (row, x * NZ + zof(d))
    meet([xdev(right), xdev(left), xdev(across)] + [zdev(d) for d in range(1, NZ)])
    started = []

    def go(src, dst, send_sem, recv_sem, peer):
        copy = remote(src, dst, send_sem, recv_sem, peer)
        copy.start()
        started.append(copy)

    def arrived(dst, send_sem, recv_sem):
        remote(dst, dst, send_sem, recv_sem, xdev(right)).wait_recv()

    for q in range(4):
        da, db = HALF_A[q], HALF_B[q]
        go(u_ref.at[across, zof(da)], from_l_relay.at[q], s_raw_r.at[q], r_relay_l.at[q], xdev(right))
        go(u_ref.at[across, zof(db)], from_r_relay.at[q], s_raw_l.at[q], r_relay_r.at[q], xdev(left))
        go(u_ref.at[right, zof(db)], in_l.at[db], s_raw_r.at[4 + q], r_in_l.at[db], xdev(right))
        go(u_ref.at[left, zof(da)], in_r.at[da], s_raw_l.at[4 + q], r_in_r.at[da], xdev(left))
    for q in range(4):
        da, db = HALF_A[q], HALF_B[q]
        arrived(from_l_relay.at[q], s_raw_r.at[q], r_relay_l.at[q])
        to_r[q] = (from_l_relay[q].astype(F32) + u_ref[right, zof(da)].astype(F32)).astype(BF16)
        go(to_r.at[q], in_l.at[da], s_mix_r.at[q], r_in_l.at[da], xdev(right))
        arrived(from_r_relay.at[q], s_raw_l.at[q], r_relay_r.at[q])
        to_l[q] = (from_r_relay[q].astype(F32) + u_ref[left, zof(db)].astype(F32)).astype(BF16)
        go(to_l.at[q], in_r.at[db], s_mix_l.at[q], r_in_r.at[db], xdev(left))

    def xsum(d):
        arrived(in_l.at[d], s_raw_r.at[0], r_in_l.at[d])
        arrived(in_r.at[d], s_raw_r.at[0], r_in_r.at[d])
        return u_ref[x, zof(d)].astype(F32) + in_l[d].astype(F32) + in_r[d].astype(F32)

    for d in (4, 5, 3, 6, 2, 7, 1):
        summed[d] = xsum(d).astype(BF16)
        go(summed.at[d], zin.at[d], s_z.at[d], r_z.at[d], zdev(d))
    total = xsum(0)
    for d in (1, 7, 2, 6, 3, 5, 4):
        arrived(zin.at[d], s_z.at[d], r_z.at[d])
        total = total + zin[d].astype(F32)

    ut = total.astype(BF16)
    un = total.T.astype(BF16)
    pre = jnp.dot(un, w_ref[...], preferred_element_type=F32) + bias_ref[...]
    s = jax.nn.sigmoid(pre)
    grad = (cot_ref[...] * s * (1.0 + pre * (1.0 - s))).astype(BF16)
    own[...] = grad
    act_ref[...] = pre * s

    for d in (4, 3, 5, 2, 6, 1, 7):
        go(own, band_ref.at[x, z], s_gz.at[d], r_gz.at[d], zdev(d))
    go(own, band_ref.at[x, z], s_gr.at[0], r_gl.at[0], xdev(right))
    go(own, band_ref.at[x, z], s_gl.at[0], r_gr.at[0], xdev(left))
    band_ref[x, z] = grad

    gw = jnp.dot(ut, grad, preferred_element_type=F32)
    wbuf[0:16] = gw.reshape(16, 8, T)
    gb = jnp.sum(grad.astype(F32), axis=0, keepdims=True)
    wbuf[16] = jnp.broadcast_to(gb, (8, T))
    wbuf[17:32] = jnp.zeros((15, 8, T), F32)
    for e in (2, 1, 3):
        xx = lax.rem(x + e, NX)
        go(wbuf.at[pl.ds(xx * NZ, NZ)], wxin.at[e], s_wx.at[e], r_wx.at[e], xdev(xx))

    order = (0, 1, 7, 2, 6, 3, 5, 4)
    half_a = (0, 7, 6, 5)

    def relay(d):
        zz = zfrom(d)
        arrived(band_ref.at[left, zz], s_gr.at[0], r_gl.at[d])
        if d in half_a:
            go(band_ref.at[left, zz], band_ref.at[left, zz], s_rel.at[d], r_rel.at[d], xdev(right))
        arrived(band_ref.at[right, zz], s_gr.at[0], r_gr.at[d])
        if d not in half_a:
            go(band_ref.at[right, zz], band_ref.at[right, zz], s_rel.at[d], r_rel.at[d], xdev(left))

    def weight_x():
        acc = wbuf[pl.ds(x * NZ, NZ)]
        for e in (1, 3, 2):
            arrived(wxin.at[e], s_wx.at[e], r_wx.at[e])
            acc = acc + wxin[e]
        wz[...] = acc
        for d in (4, 3, 5, 2, 6, 1, 7):
            go(wz.at[zof(d)], wzin.at[d], s_wz.at[d], r_wz.at[d], zdev(d))

    for n, d in enumerate(order):
        if d:
            zz = zfrom(d)
            arrived(band_ref.at[x, zz], s_gz.at[d], r_gz.at[d])
            go(band_ref.at[x, zz], band_ref.at[x, zz], s_gr.at[d], r_gl.at[d], xdev(right))
            go(band_ref.at[x, zz], band_ref.at[x, zz], s_gl.at[d], r_gr.at[d], xdev(left))
        if n == 2:
            weight_x()
        if n >= 2:
            relay(order[n - 2])
    relay(order[-2])
    relay(order[-1])
    wtotal = wz[z]
    for d in (1, 7, 2, 6, 3, 5, 4):
        arrived(wzin.at[d], s_wz.at[d], r_wz.at[d])
        wtotal = wtotal + wzin[d]
    wsum_ref[...] = wtotal
    for d in order:
        arrived(band_ref.at[across, zfrom(d)], s_rel.at[d], r_rel.at[d])
    for copy in started:
        copy.wait_send()


def last_kernel(
    f_ref, wchunk_ref, out_ref, wout_ref,
    pin, sbuf, yin, wpin, wp, wyin, wt,
    s_p, r_p, s_y, r_y, s_wp, r_wp, s_wy, r_wy, s_wz, r_wz, s_wx, r_wx,
):
    row, col, y, k, x, z = place()
    partner = (y * NK + 1 - k, col)
    yof = lambda d: lax.rem(y + d, NY)
    ydev = lambda d: (yof(d) * NK + k, col)
    zdev = lambda d: (row, x * NZ + lax.rem(z + d, NZ))
    xdev = lambda e: (row, lax.rem(x + e, NX) * NZ + z)
    meet([partner] + [ydev(d) for d in range(1, NY)] + [zdev(d) for d in range(1, NZ)] + [xdev(e) for e in range(1, NX)])
    started = []

    def go(src, dst, send_sem, recv_sem, peer):
        copy = remote(src, dst, send_sem, recv_sem, peer)
        copy.start()
        started.append(copy)

    def arrived(dst, send_sem, recv_sem):
        remote(dst, dst, send_sem, recv_sem, partner).wait_recv()

    order = (4, 3, 5, 2, 6, 1, 7)
    near = (1, 7, 2, 6, 3, 5, 4)
    go(wchunk_ref, wpin, s_wp, r_wp, partner)
    for d in order + (0,):
        go(f_ref.at[yof(d), 1 - k], pin.at[d], s_p.at[d], r_p.at[d], partner)
    arrived(wpin, s_wp, r_wp)
    wpair = wchunk_ref[...] + wpin[...]
    wp[...] = wpair
    for d in order:
        go(wp, wyin.at[d], s_wy.at[d], r_wy.at[d], ydev(d))
    for d in order:
        arrived(pin.at[d], s_p.at[d], r_p.at[d])
        sbuf[d] = (pin[d].astype(F32) + f_ref[yof(d), k].astype(F32)).astype(BF16)
        go(sbuf.at[d], yin.at[d], s_y.at[d], r_y.at[d], ydev(d))
    arrived(pin.at[0], s_p.at[0], r_p.at[0])
    total = pin[0].astype(F32) + f_ref[y, k].astype(F32)

    wtotal = wpair
    for d in near:
        arrived(wyin.at[d], s_wy.at[d], r_wy.at[d])
        wtotal = wtotal + wyin[d]
    wt[...] = wtotal
    for d in order:
        go(wt, wout_ref.at[x, z], s_wz.at[d], r_wz.at[d], zdev(d))
    wout_ref[x, z] = wtotal

    for d in near:
        arrived(yin.at[d], s_y.at[d], r_y.at[d])
        total = total + yin[d].astype(F32)
    out_ref[...] = total.astype(BF16)

    for d in near:
        arrived(wout_ref.at[x, lax.rem(z + NZ - d, NZ)], s_wz.at[d], r_wz.at[d])
    for e in (2, 1, 3):
        go(wout_ref.at[x], wout_ref.at[x], s_wx.at[e], r_wx.at[e], xdev(e))
    for e in (1, 3, 2):
        arrived(wout_ref.at[lax.rem(x + NX - e, NX)], s_wx.at[e], r_wx.at[e])
    for copy in started:
        copy.wait_send()


def dma(*shape):
    return pltpu.SemaphoreType.DMA(shape)


def params(collective):
    return pltpu.CompilerParams(collective_id=collective, has_side_effects=True)


def shards(features, weight, bias_vector, tile_rows, tile_cols, neighbours, edge_weights, tile_count, cotangent):
    nodes, width = features.shape
    rows_here = tile_rows[0, 0]
    cols_here = tile_cols[0, 0]
    ids_here = neighbours[0, 0]
    values_here = edge_weights[0, 0]
    count = tile_count[0]
    groups = NY * NK
    block = jax.ShapeDtypeStruct
    hidden = weight.shape[1]

    gathered = pl.pallas_call(
        gather_kernel,
        out_shape=block((groups, width, nodes), BF16),
        in_specs=[VMEM_SPEC],
        out_specs=VMEM_SPEC,
        scratch_shapes=[dma(NY), dma(NY), dma(NY), dma(NY)],
        compiler_params=params(0),
        name="gather_features",
    )(features.T)
    panel = gathered.reshape(groups * width, nodes)

    partial = pl.pallas_call(
        functools.partial(forward_kernel, 4),
        out_shape=block((NX * NZ, T, T), BF16),
        in_specs=[SMEM_SPEC] * 3 + [VMEM_SPEC] * 3,
        out_specs=VMEM_SPEC,
        scratch_shapes=[pltpu.VMEM((NX * NZ, T, T), F32)],
        name="forward_tiles",
    )(rows_here, cols_here, count, panel, ids_here, values_here)

    vbf = lambda *shape: pltpu.VMEM(shape, BF16)
    vf = lambda *shape: pltpu.VMEM(shape, F32)
    activations, band, wchunk = pl.pallas_call(
        middle_kernel,
        out_shape=(block((T, hidden), F32), block((NX, NZ, T, hidden), BF16), block((8, hidden), F32)),
        in_specs=[VMEM_SPEC] * 4,
        out_specs=(VMEM_SPEC,) * 3,
        scratch_shapes=[
            vbf(4, T, T), vbf(4, T, T), vbf(4, T, T), vbf(4, T, T),
            vbf(NZ, T, T), vbf(NZ, T, T), vbf(NZ, T, T), vbf(NZ, T, T), vbf(T, T),
            vf(NX * NZ, 8, T), vf(NX, NZ, 8, T), vf(NZ, 8, T), vf(NZ, 8, T),
            dma(8), dma(8), dma(4), dma(4), dma(4), dma(4), dma(NZ), dma(NZ),
            dma(NZ), dma(NZ), dma(NZ), dma(NZ), dma(NZ), dma(NZ), dma(NZ), dma(NZ), dma(NZ), dma(NZ),
            dma(NX), dma(NX), dma(NZ), dma(NZ),
        ],
        compiler_params=params(1),
        name="middle",
    )(partial.reshape(NX, NZ, T, T), weight, bias_vector.reshape(1, hidden), cotangent)

    terms = pl.pallas_call(
        functools.partial(backward_kernel, 4),
        out_shape=block((groups * width, nodes), BF16),
        in_specs=[SMEM_SPEC] * 3 + [VMEM_SPEC] * 4,
        out_specs=VMEM_SPEC,
        scratch_shapes=[vf(nodes // T, T, hidden)],
        name="backward_tiles",
    )(rows_here, cols_here, count, band.reshape(NX * NZ, T, hidden), weight, ids_here, values_here)

    grad_t, wgrad = pl.pallas_call(
        last_kernel,
        out_shape=(block((width, nodes), BF16), block((NX, NZ, 8, hidden), F32)),
        in_specs=[VMEM_SPEC] * 2,
        out_specs=(VMEM_SPEC,) * 2,
        scratch_shapes=[
            vbf(NY, width, nodes), vbf(NY, width, nodes), vbf(NY, width, nodes),
            vf(8, hidden), vf(8, hidden), vf(NY, 8, hidden), vf(8, hidden),
            dma(NY), dma(NY), dma(NY), dma(NY), dma(), dma(), dma(NY), dma(NY), dma(NZ), dma(NZ), dma(NX), dma(NX),
        ],
        compiler_params=params(2),
        name="scatter_gradients",
    )(terms.reshape(NY, NK, width, nodes), wchunk)

    node_count = cotangent.shape[0] * lax.axis_size("row") * lax.axis_size("col")
    shrink = float(node_count) ** (-0.5)
    wflat = wgrad.reshape(NX * NZ * 8, hidden) * shrink
    return activations, grad_t.T, wflat[: weight.shape[0]], wflat[weight.shape[0]]


def solution(mesh):
    in_specs = (
        P("col", "row"),
        P(),
        P(),
        P("row", "col", None),
        P("row", "col", None),
        P("row", "col", None, None, None),
        P("row", "col", None, None, None),
        P("row", "col"),
        P(("row", "col"), None),
    )
    out_specs = (P(("row", "col"), None), P("col", "row"), P(), P())
    return jax.shard_map(shards, mesh=mesh, in_specs=in_specs, out_specs=out_specs, check_vma=False)
```

```python
import functools

import jax
import jax.numpy as jnp
from jax import lax
from jax.experimental import pallas as pl
from jax.experimental.pallas import tpu as pltpu
from jax.sharding import PartitionSpec as P

NX = 4
NZ = 8
NY = 8
NK = 2
T = 128
F32 = jnp.float32
BF16 = jnp.bfloat16
MESH = pl.DeviceIdType.MESH
VMEM_SPEC = pl.BlockSpec(memory_space=pltpu.VMEM)
SMEM_SPEC = pl.BlockSpec(memory_space=pltpu.SMEM)
HALF_A = (4, 3, 2, 1)
HALF_B = (5, 6, 7, 0)


def place():
    row = lax.axis_index("row")
    col = lax.axis_index("col")
    return row, col, row // NK, row % NK, col // NZ, col % NZ


def remote(src, dst, send_sem, recv_sem, peer):
    return pltpu.make_async_remote_copy(
        src_ref=src,
        dst_ref=dst,
        send_sem=send_sem,
        recv_sem=recv_sem,
        device_id=peer,
        device_id_type=MESH,
    )


def tile_matrix(t, live, nb_ref, ew_ref, rows_iota):
    ids = nb_ref[t]
    values = ew_ref[t].astype(F32)
    values = jnp.where(live, values, jnp.zeros_like(values))
    second = jnp.where(rows_iota == ids[1:2, :], values[1:2, :], 0.0)
    return jnp.where(rows_iota == ids[0:1, :], values[0:1, :], second).astype(BF16)


def links(blocks_row, tiles):
    across = jnp.broadcast_to(blocks_row, (tiles, tiles))
    down = across.T
    first = lax.broadcasted_iota(jnp.int32, (tiles, tiles), 0)
    second = lax.broadcasted_iota(jnp.int32, (tiles, tiles), 1)
    before = jnp.max(jnp.where((down == across) & (first < second), first, -1), axis=0, keepdims=True)
    last = jnp.max(jnp.where(down == second, first, -1), axis=0, keepdims=True)
    pick = lambda v: jnp.minimum(jnp.where(v < 0, tiles, v), tiles)
    return pick(before), pick(last)


def whole_kernel(
    rows_ref, cols_ref, count_ref, rows_vec, cols_vec, ft_ref, nb_ref, ew_ref, w_ref, bias_ref, cot_ref,
    act_ref, grad_ref, wout_ref,
    dense, prefix, table_v, table, ftraw, panel, u_ref, band_ref, fbuf,
    from_l_relay, from_r_relay, to_r, to_l, in_l, in_r, summed, zin, own,
    wbuf, wxin, wz, wzin, wcol, wpin, wp, wyin, wt,
    pin, sbuf, yin,
    s_tab, s_fy, r_fy, s_fp, r_fp,
    s_raw_r, s_raw_l, s_mix_r, s_mix_l, r_relay_l, r_relay_r, r_in_l, r_in_r,
    s_z, r_z, s_gz, r_gz, s_gr, s_gl, r_gl, r_gr, s_rel, r_rel, s_wx, r_wx, s_wz, r_wz,
    s_p, r_p, s_y, r_y, s_wp, r_wp, s_wy, r_wy, s_oz, r_oz, s_ox, r_ox,
):
    row, col, y, k, x, z = place()
    tiles = nb_ref.shape[0]
    right = lax.rem(x + 1, NX)
    left = lax.rem(x + NX - 1, NX)
    across = lax.rem(x + 2, NX)
    xdev = lambda xx: (row, xx * NZ + z)
    zof = lambda d: lax.rem(z + d, NZ)
    zfrom = lambda d: lax.rem(z + NZ - d, NZ)
    zdev = lambda d: (row, x * NZ + zof(d))
    partner = (y * NK + 1 - k, col)
    yof = lambda d: lax.rem(y + d, NY)
    ydev = lambda d: (yof(d) * NK + k, col)
    far = (4, 3, 5, 2, 6, 1, 7)
    near = (1, 7, 2, 6, 3, 5, 4)
    peers = [partner] + [ydev(d) for d in range(1, NY)]
    peers += [xdev(right), xdev(left), xdev(across)] + [zdev(d) for d in range(1, NZ)]
    started = []

    def go(src, dst, send_sem, recv_sem, peer):
        copy = remote(src, dst, send_sem, recv_sem, peer)
        copy.start()
        started.append(copy)

    def arrived(dst, send_sem, recv_sem):
        remote(dst, dst, send_sem, recv_sem, partner).wait_recv()

    barrier = pltpu.get_barrier_semaphore()
    for peer in peers:
        pl.semaphore_signal(barrier, inc=1, device_id=peer, device_id_type=MESH)

    row_before, row_last = links(rows_vec[...], tiles)
    col_before, col_last = links(cols_vec[...], tiles)
    table_v[0:1, :] = row_before
    table_v[1:2, :] = row_last
    table_v[2:3, :] = col_before
    table_v[3:4, :] = col_last
    table_v[4:8, :] = jnp.zeros((4, tiles), jnp.int32)
    to_smem = pltpu.make_async_copy(table_v, table, s_tab)
    to_smem.start()
    count = count_ref[0]
    iota = lax.broadcasted_iota(jnp.int32, (T, T), 0)

    def build(g, carry):
        for u in range(4):
            t = g * 4 + u
            dense[t] = tile_matrix(t, t < count, nb_ref, ew_ref, iota)
        return carry

    lax.fori_loop(0, tiles // 4, build, 0)
    prefix[tiles] = jnp.zeros((T, T), F32)
    pl.semaphore_wait(barrier, len(peers))

    for d in far:
        go(ft_ref, ftraw.at[row], s_fy.at[d], r_fy.at[d], ydev(d))
    go(ft_ref, ftraw.at[row], s_fp.at[0], r_fp.at[0], partner)
    ftraw[row] = ft_ref[...]
    to_smem.wait()
    for d in near:
        slot = lax.rem(y + NY - d, NY) * NK + k
        arrived(ftraw.at[slot], s_fy.at[d], r_fy.at[d])
        go(ftraw.at[slot], ftraw.at[slot], s_fp.at[d], r_fp.at[d], partner)
    for d in (0,) + near:
        arrived(ftraw.at[lax.rem(y + NY - d, NY) * NK + 1 - k], s_fp.at[d], r_fp.at[d])
    for c in range(NX * NZ // 2):
        wide = ftraw[:, :, c * T : (c + 1) * T].astype(F32)
        panel[c] = wide.reshape(T, T).astype(BF16)

    def forward(g, carry):
        for u in range(4):
            t = g * 4 + u
            prod = jnp.dot(panel[cols_ref[t]], dense[t], preferred_element_type=F32)
            prefix[t] = prefix[table[0, t]] + prod
        return carry

    lax.fori_loop(0, tiles // 4, forward, 0)

    def block_row(xx, d):
        u_ref[xx, zof(d)] = prefix[table[1, xx * NZ + zof(d)]].astype(BF16)

    for d in HALF_A + HALF_B:
        block_row(across, d)
    for q in range(4):
        da, db = HALF_A[q], HALF_B[q]
        go(u_ref.at[across, zof(da)], from_l_relay.at[q], s_raw_r.at[q], r_relay_l.at[q], xdev(right))
        go(u_ref.at[across, zof(db)], from_r_relay.at[q], s_raw_l.at[q], r_relay_r.at[q], xdev(left))
    for d in HALF_A + HALF_B:
        block_row(right, d)
        block_row(left, d)
        block_row(x, d)
    for q in range(4):
        da, db = HALF_A[q], HALF_B[q]
        arrived(from_l_relay.at[q], s_raw_r.at[q], r_relay_l.at[q])
        to_r[q] = (from_l_relay[q].astype(F32) + u_ref[right, zof(da)].astype(F32)).astype(BF16)
        arrived(from_r_relay.at[q], s_raw_l.at[q], r_relay_r.at[q])
        to_l[q] = (from_r_relay[q].astype(F32) + u_ref[left, zof(db)].astype(F32)).astype(BF16)
        go(to_r.at[q], in_l.at[da], s_mix_r.at[q], r_in_l.at[da], xdev(right))
        go(to_l.at[q], in_r.at[db], s_mix_l.at[q], r_in_r.at[db], xdev(left))
        go(u_ref.at[right, zof(db)], in_l.at[db], s_raw_r.at[4 + q], r_in_l.at[db], xdev(right))
        go(u_ref.at[left, zof(da)], in_r.at[da], s_raw_l.at[4 + q], r_in_r.at[da], xdev(left))

    def xsum(d):
        arrived(in_l.at[d], s_raw_r.at[0], r_in_l.at[d])
        arrived(in_r.at[d], s_raw_r.at[0], r_in_r.at[d])
        return u_ref[x, zof(d)].astype(F32) + in_l[d].astype(F32) + in_r[d].astype(F32)

    for d in (4, 5, 3, 6, 2, 7, 1):
        summed[d] = xsum(d).astype(BF16)
        go(summed.at[d], zin.at[d], s_z.at[d], r_z.at[d], zdev(d))
    total = xsum(0)
    for d in near:
        arrived(zin.at[d], s_z.at[d], r_z.at[d])
        total = total + zin[d].astype(F32)

    ut = total.astype(BF16)
    un = total.T
    un_high = un.astype(BF16)
    un_low = (un - un_high.astype(F32)).astype(BF16)
    pre = jnp.dot(un_high, w_ref[...], preferred_element_type=F32) + bias_ref[...]
    pre = pre + jnp.dot(un_low, w_ref[...], preferred_element_type=F32)
    s = jax.nn.sigmoid(pre)
    grad = (cot_ref[...] * s * (1.0 + pre * (1.0 - s))).astype(BF16)
    own[...] = grad

    for d in far:
        go(own, band_ref.at[x, z], s_gz.at[d], r_gz.at[d], zdev(d))
    go(own, band_ref.at[x, z], s_gr.at[0], r_gl.at[0], xdev(right))
    go(own, band_ref.at[x, z], s_gl.at[0], r_gr.at[0], xdev(left))
    band_ref[x, z] = grad
    act_ref[...] = pre * s

    gw = jnp.dot(ut, grad, preferred_element_type=F32)
    wbuf[0:16] = gw.reshape(16, 8, T)
    gb = jnp.sum(grad.astype(F32), axis=0, keepdims=True)
    wbuf[16] = jnp.broadcast_to(gb, (8, T))
    wbuf[17:32] = jnp.zeros((15, 8, T), F32)

    half_a = (0, 7, 6, 5)

    def spread(d):
        zz = zfrom(d)
        arrived(band_ref.at[x, zz], s_gz.at[d], r_gz.at[d])
        go(band_ref.at[x, zz], band_ref.at[x, zz], s_gr.at[d], r_gl.at[d], xdev(right))
        go(band_ref.at[x, zz], band_ref.at[x, zz], s_gl.at[d], r_gr.at[d], xdev(left))

    def relay(d):
        zz = zfrom(d)
        arrived(band_ref.at[left, zz], s_gr.at[0], r_gl.at[d])
        if d in half_a:
            go(band_ref.at[left, zz], band_ref.at[left, zz], s_rel.at[d], r_rel.at[d], xdev(right))
        arrived(band_ref.at[right, zz], s_gr.at[0], r_gr.at[d])
        if d not in half_a:
            go(band_ref.at[right, zz], band_ref.at[right, zz], s_rel.at[d], r_rel.at[d], xdev(left))

    for d in (1, 7, 2, 6):
        spread(d)
    relay(0)
    spread(3)
    relay(1)
    spread(5)
    relay(7)
    spread(4)
    for e in (2, 1, 3):
        xx = lax.rem(x + e, NX)
        go(wbuf.at[pl.ds(xx * NZ, NZ)], wxin.at[e], s_wx.at[e], r_wx.at[e], xdev(xx))
    for d in (2, 6, 3, 5, 4):
        relay(d)
    wsum = wbuf[pl.ds(x * NZ, NZ)]
    for e in (1, 3, 2):
        arrived(wxin.at[e], s_wx.at[e], r_wx.at[e])
        wsum = wsum + wxin[e]
    wz[...] = wsum
    for d in far:
        go(wz.at[zof(d)], wzin.at[d], s_wz.at[d], r_wz.at[d], zdev(d))
    for d in (0,) + near:
        arrived(band_ref.at[across, zfrom(d)], s_rel.at[d], r_rel.at[d])

    def backward(g, carry):
        for u in range(4):
            t = g * 4 + u
            r = rows_ref[t]
            prod = jnp.dot(dense[t], band_ref[r // NZ, r % NZ], preferred_element_type=F32)
            prefix[t] = prefix[table[2, t]] + prod
        return carry

    lax.fori_loop(0, tiles // 16, backward, 0)
    wtotal = wz[z]
    for d in near:
        arrived(wzin.at[d], s_wz.at[d], r_wz.at[d])
        wtotal = wtotal + wzin[d]
    wcol[...] = wtotal
    go(wcol, wpin, s_wp, r_wp, partner)
    lax.fori_loop(tiles // 16, tiles // 8, backward, 0)
    arrived(wpin, s_wp, r_wp)
    wpair = wtotal + wpin[...]
    wp[...] = wpair
    for d in far:
        go(wp, wyin.at[d], s_wy.at[d], r_wy.at[d], ydev(d))
    lax.fori_loop(tiles // 8, tiles // 4, backward, 0)

    contract = (((1,), (1,)), ((), ()))
    for c in range(fbuf.shape[3] // T):
        value = prefix[table[3, c]]
        high = value.astype(BF16)
        low = (value - high.astype(F32)).astype(BF16)
        term = lax.dot_general(w_ref[...], high, contract, preferred_element_type=F32)
        term += lax.dot_general(w_ref[...], low, contract, preferred_element_type=F32)
        fbuf[:, :, :, c * T : (c + 1) * T] = term.reshape(NY, NK, 8, T)

    for d in far + (0,):
        go(fbuf.at[yof(d), 1 - k], pin.at[d], s_p.at[d], r_p.at[d], partner)
    wtotal = wpair
    for d in near:
        arrived(wyin.at[d], s_wy.at[d], r_wy.at[d])
        wtotal = wtotal + wyin[d]
    wt[...] = wtotal
    for d in far:
        arrived(pin.at[d], s_p.at[d], r_p.at[d])
        sbuf[d] = (pin[d] + fbuf[yof(d), k]).astype(BF16)
        go(sbuf.at[d], yin.at[d], s_y.at[d], r_y.at[d], ydev(d))
    for d in far:
        go(wt, wout_ref.at[x, z], s_oz.at[d], r_oz.at[d], zdev(d))
    wout_ref[x, z] = wtotal
    arrived(pin.at[0], s_p.at[0], r_p.at[0])
    total = pin[0] + fbuf[y, k]
    for d in near:
        arrived(wout_ref.at[x, zfrom(d)], s_oz.at[d], r_oz.at[d])
    for e in (2, 1, 3):
        go(wout_ref.at[x], wout_ref.at[x], s_ox.at[e], r_ox.at[e], xdev(lax.rem(x + e, NX)))
    for d in near:
        arrived(yin.at[d], s_y.at[d], r_y.at[d])
        total = total + yin[d].astype(F32)
    grad_ref[...] = total.astype(BF16)
    for e in (1, 3, 2):
        arrived(wout_ref.at[lax.rem(x + NX - e, NX)], s_ox.at[e], r_ox.at[e])
    for copy in started:
        copy.wait_send()


def finish_kernel(shrink, act_ref, grad_ref, w_ref, act_out, grad_out, w_out, b_out):
    act_out[...] = act_ref[...]
    grad_out[...] = grad_ref[...]
    w_out[...] = w_ref[0:16].reshape(16 * 8, T) * shrink
    b_out[...] = w_ref[16][0:1, :] * shrink


def dma(*shape):
    return pltpu.SemaphoreType.DMA(shape)


def shards(features, weight, bias_vector, tile_rows, tile_cols, neighbours, edge_weights, tile_count, cotangent):
    nodes, width = features.shape
    rows_here = tile_rows[0, 0]
    cols_here = tile_cols[0, 0]
    hidden = weight.shape[1]
    tiles = neighbours.shape[2]
    shape = jax.ShapeDtypeStruct
    vbf = lambda *dims: pltpu.VMEM(dims, BF16)
    vf = lambda *dims: pltpu.VMEM(dims, F32)

    act, grad_t, wall = pl.pallas_call(
        whole_kernel,
        out_shape=(shape((T, hidden), F32), shape((width, nodes), BF16), shape((NX, NZ, 8, hidden), F32)),
        in_specs=[SMEM_SPEC] * 3 + [VMEM_SPEC] * 8,
        out_specs=(VMEM_SPEC,) * 3,
        scratch_shapes=[
            vbf(tiles, T, T), vf(tiles + 1, T, T), pltpu.VMEM((8, tiles), jnp.int32), pltpu.SMEM((8, tiles), jnp.int32),
            vbf(NY * NK, width, nodes), vbf(nodes // T, T, T), vbf(NX, NZ, T, T), vbf(NX, NZ, T, T),
            vf(NY, NK, width, nodes),
            vbf(4, T, T), vbf(4, T, T), vbf(4, T, T), vbf(4, T, T),
            vbf(NZ, T, T), vbf(NZ, T, T), vbf(NZ, T, T), vbf(NZ, T, T), vbf(T, T),
            vf(NX * NZ, 8, T), vf(NX, NZ, 8, T), vf(NZ, 8, T), vf(NZ, 8, T),
            vf(8, T), vf(8, T), vf(8, T), vf(NY, 8, T), vf(8, T),
            vf(NY, width, nodes), vbf(NY, width, nodes), vbf(NY, width, nodes),
            dma(), dma(NY), dma(NY), dma(NY), dma(NY),
            dma(8), dma(8), dma(4), dma(4), dma(4), dma(4), dma(NZ), dma(NZ),
            dma(NZ), dma(NZ), dma(NZ), dma(NZ), dma(NZ), dma(NZ), dma(NZ), dma(NZ), dma(NZ), dma(NZ),
            dma(NX), dma(NX), dma(NZ), dma(NZ),
            dma(NY), dma(NY), dma(NY), dma(NY), dma(), dma(), dma(NY), dma(NY), dma(NZ), dma(NZ), dma(NX), dma(NX),
        ],
        compiler_params=pltpu.CompilerParams(collective_id=0, has_side_effects=True, vmem_limit_bytes=32 << 20),
        name="whole",
    )(
        rows_here, cols_here, tile_count[0], tile_rows[0], tile_cols[0], features.T,
        neighbours[0, 0], edge_weights[0, 0], weight, bias_vector.reshape(1, hidden), cotangent,
    )

    node_count = cotangent.shape[0] * lax.axis_size("row") * lax.axis_size("col")
    shrink = float(node_count) ** (-0.5)
    act, grad_t, wgrad, bgrad = pl.pallas_call(
        functools.partial(finish_kernel, shrink),
        out_shape=(
            shape((T, hidden), F32), shape((width, nodes), BF16), shape((T, hidden), F32), shape((1, hidden), F32),
        ),
        in_specs=[VMEM_SPEC] * 3,
        out_specs=(VMEM_SPEC,) * 4,
        compiler_params=pltpu.CompilerParams(vmem_limit_bytes=4 << 20),
        name="finish",
    )(act, grad_t, wall.reshape(NX * NZ, 8, hidden))
    return act, grad_t.T, wgrad, bgrad.reshape(hidden)


def solution(mesh):
    in_specs = (
        P("col", "row"),
        P(),
        P(),
        P("row", "col", None),
        P("row", "col", None),
        P("row", "col", None, None, None),
        P("row", "col", None, None, None),
        P("row", "col"),
        P(("row", "col"), None),
    )
    out_specs = (P(("row", "col"), None), P("col", "row"), P(), P())
    return jax.shard_map(shards, mesh=mesh, in_specs=in_specs, out_specs=out_specs, check_vma=False)
```

```python
import functools

import jax
import jax.numpy as jnp
from jax import lax
from jax.experimental import pallas as pl
from jax.experimental.pallas import tpu as pltpu
from jax.sharding import PartitionSpec as P

NX = 4
NZ = 8
NY = 8
NK = 2
T = 128
STEP = 8
F32 = jnp.float32
BF16 = jnp.bfloat16
MESH = pl.DeviceIdType.MESH
VMEM_SPEC = pl.BlockSpec(memory_space=pltpu.VMEM)
HBM_SPEC = pl.BlockSpec(memory_space=pltpu.HBM)
HALF_A = (4, 3, 2, 1)
HALF_B = (5, 6, 7, 0)


def place():
    row = lax.axis_index("row")
    col = lax.axis_index("col")
    return row, col, row // NK, row % NK, col // NZ, col % NZ


def remote(src, dst, send_sem, recv_sem, peer):
    return pltpu.make_async_remote_copy(
        src_ref=src,
        dst_ref=dst,
        send_sem=send_sem,
        recv_sem=recv_sem,
        device_id=peer,
        device_id_type=MESH,
    )


def tile_matrix(t, live, nb_ref, ew_ref, rows_iota):
    ids = nb_ref[t]
    values = ew_ref[t].astype(F32)
    values = jnp.where(live, values, jnp.zeros_like(values))
    second = jnp.where(rows_iota == ids[1:2, :], values[1:2, :], 0.0)
    return jnp.where(rows_iota == ids[0:1, :], values[0:1, :], second).astype(BF16)


def links(blocks_row, tiles):
    across = jnp.broadcast_to(blocks_row, (tiles, tiles))
    down = across.T
    first = lax.broadcasted_iota(jnp.int32, (tiles, tiles), 0)
    second = lax.broadcasted_iota(jnp.int32, (tiles, tiles), 1)
    before = jnp.max(jnp.where((down == across) & (first < second), first, -1), axis=0, keepdims=True)
    last = jnp.max(jnp.where(down == second, first, -1), axis=0, keepdims=True)
    pick = lambda v: jnp.minimum(jnp.where(v < 0, tiles, v), tiles)
    return pick(before), pick(last)


def whole_kernel(
    rows_hbm, cols_hbm, count_hbm, ft_hbm, nb_hbm, ew_hbm, w_hbm, bias_hbm, cot_hbm,
    act_ref, grad_ref, wout_ref,
    rows_ref, cols_ref, count_ref, rows_vec, cols_vec, nb_ref, ew_ref, w_ref, bias_ref, cot_ref, s_in,
    dense, prefix, table_v, table, ftraw, panel, u_ref, band_ref, fbuf,
    from_l_relay, from_r_relay, to_r, to_l, in_l, in_r, summed, zin, own,
    act_v, grad_v, wall, s_out, wbuf, wxin, wx, wzin, wcol, wpin, wp, wyin, wt,
    pin, sbuf, yin,
    s_tab, s_fy, r_fy, s_fp, r_fp,
    s_raw_r, s_raw_l, s_mix_r, s_mix_l, r_relay_l, r_relay_r, r_in_l, r_in_r,
    s_z, r_z, s_gz, r_gz, s_gr, s_gl, r_gl, r_gr, s_rel, r_rel, s_wx, r_wx, s_wz, r_wz,
    s_p, r_p, s_y, r_y, s_wp, r_wp, s_wy, r_wy, s_oz, r_oz, s_ox, r_ox,
):
    row, col, y, k, x, z = place()
    tiles = nb_ref.shape[0]
    right = lax.rem(x + 1, NX)
    left = lax.rem(x + NX - 1, NX)
    across = lax.rem(x + 2, NX)
    xdev = lambda xx: (row, xx * NZ + z)
    zof = lambda d: lax.rem(z + d, NZ)
    zfrom = lambda d: lax.rem(z + NZ - d, NZ)
    zdev = lambda d: (row, x * NZ + zof(d))
    partner = (y * NK + 1 - k, col)
    yof = lambda d: lax.rem(y + d, NY)
    ydev = lambda d: (yof(d) * NK + k, col)
    far = (4, 3, 5, 2, 6, 1, 7)
    near = (1, 7, 2, 6, 3, 5, 4)
    peers = [partner] + [ydev(d) for d in range(1, NY)]
    peers += [xdev(right), xdev(left), xdev(across)] + [zdev(d) for d in range(1, NZ)]
    started = []

    def go(src, dst, send_sem, recv_sem, peer):
        copy = remote(src, dst, send_sem, recv_sem, peer)
        copy.start()
        started.append(copy)

    def arrived(dst, send_sem, recv_sem):
        remote(dst, dst, send_sem, recv_sem, partner).wait_recv()

    def drain():
        for copy in started:
            copy.wait_send()
        started.clear()

    barrier = pltpu.get_barrier_semaphore()
    for peer in peers:
        pl.semaphore_signal(barrier, inc=1, device_id=peer, device_id_type=MESH)

    pairs = (
        (rows_hbm, rows_vec), (cols_hbm, cols_vec), (nb_hbm, nb_ref), (ew_hbm, ew_ref), (count_hbm, count_ref),
        (ft_hbm, ftraw.at[row]), (rows_hbm, rows_ref), (cols_hbm, cols_ref), (w_hbm, w_ref), (bias_hbm, bias_ref),
        (cot_hbm, cot_ref),
    )
    loads = [pltpu.make_async_copy(src, dst, s_in.at[n]) for n, (src, dst) in enumerate(pairs)]
    for load in loads:
        load.start()
    loads[0].wait()
    loads[1].wait()
    row_before, row_last = links(rows_vec[...], tiles)
    col_before, col_last = links(cols_vec[...], tiles)
    table_v[0:1, :] = row_before
    table_v[1:2, :] = row_last
    table_v[2:3, :] = col_before
    table_v[3:4, :] = col_last
    table_v[4:8, :] = jnp.zeros((4, tiles), jnp.int32)
    to_smem = pltpu.make_async_copy(table_v, table, s_tab)
    to_smem.start()
    for load in loads[2:]:
        load.wait()
    count = count_ref[0, 0]
    iota = lax.broadcasted_iota(jnp.int32, (T, T), 0)

    def build(g, carry):
        for u in range(4):
            t = g * 4 + u
            dense[t] = tile_matrix(t, t < count, nb_ref, ew_ref, iota)
        return carry

    lax.fori_loop(0, tiles // 4, build, 0)
    prefix[tiles] = jnp.zeros((T, T), F32)
    pl.semaphore_wait(barrier, len(peers))

    for d in far:
        go(ftraw.at[row], ftraw.at[row], s_fy.at[d], r_fy.at[d], ydev(d))
    go(ftraw.at[row], ftraw.at[row], s_fp.at[0], r_fp.at[0], partner)
    to_smem.wait()
    for d in near:
        slot = lax.rem(y + NY - d, NY) * NK + k
        arrived(ftraw.at[slot], s_fy.at[d], r_fy.at[d])
        go(ftraw.at[slot], ftraw.at[slot], s_fp.at[d], r_fp.at[d], partner)
    for d in (0,) + near:
        arrived(ftraw.at[lax.rem(y + NY - d, NY) * NK + 1 - k], s_fp.at[d], r_fp.at[d])
    for c in range(NX * NZ // 2):
        wide = ftraw[:, :, c * T : (c + 1) * T].astype(F32)
        panel[c] = wide.reshape(T, T).astype(BF16)

    def forward(g, carry):
        for u in range(STEP):
            t = g * STEP + u
            prod = jnp.dot(panel[cols_ref[0, t]], dense[t], preferred_element_type=F32)
            prefix[t] = prefix[table[0, t]] + prod
        return carry

    lax.fori_loop(0, tiles // STEP, forward, 0)

    def block_row(xx, d):
        u_ref[xx, zof(d)] = prefix[table[1, xx * NZ + zof(d)]].astype(BF16)

    for d in HALF_A + HALF_B:
        block_row(across, d)
    for q in range(4):
        da, db = HALF_A[q], HALF_B[q]
        go(u_ref.at[across, zof(da)], from_l_relay.at[q], s_raw_r.at[q], r_relay_l.at[q], xdev(right))
        go(u_ref.at[across, zof(db)], from_r_relay.at[q], s_raw_l.at[q], r_relay_r.at[q], xdev(left))
    sent = started[-8:]
    del started[-8:]
    drain()
    started.extend(sent)
    for d in HALF_A + HALF_B:
        block_row(right, d)
        block_row(left, d)
        block_row(x, d)
    for q in range(4):
        da, db = HALF_A[q], HALF_B[q]
        arrived(from_l_relay.at[q], s_raw_r.at[q], r_relay_l.at[q])
        to_r[q] = (from_l_relay[q].astype(F32) + u_ref[right, zof(da)].astype(F32)).astype(BF16)
        arrived(from_r_relay.at[q], s_raw_l.at[q], r_relay_r.at[q])
        to_l[q] = (from_r_relay[q].astype(F32) + u_ref[left, zof(db)].astype(F32)).astype(BF16)
        go(to_r.at[q], in_l.at[da], s_mix_r.at[q], r_in_l.at[da], xdev(right))
        go(to_l.at[q], in_r.at[db], s_mix_l.at[q], r_in_r.at[db], xdev(left))
        go(u_ref.at[right, zof(db)], in_l.at[db], s_raw_r.at[4 + q], r_in_l.at[db], xdev(right))
        go(u_ref.at[left, zof(da)], in_r.at[da], s_raw_l.at[4 + q], r_in_r.at[da], xdev(left))

    def xsum(d):
        arrived(in_l.at[d], s_raw_r.at[0], r_in_l.at[d])
        arrived(in_r.at[d], s_raw_r.at[0], r_in_r.at[d])
        return u_ref[x, zof(d)].astype(F32) + in_l[d].astype(F32) + in_r[d].astype(F32)

    for d in (4, 5, 3, 6, 2, 7, 1):
        summed[d] = xsum(d).astype(BF16)
        go(summed.at[d], zin.at[d], s_z.at[d], r_z.at[d], zdev(d))
    total = xsum(0)
    for d in near:
        arrived(zin.at[d], s_z.at[d], r_z.at[d])
        total = total + zin[d].astype(F32)

    ut = total.astype(BF16)
    un = total.T
    un_high = un.astype(BF16)
    un_low = (un - un_high.astype(F32)).astype(BF16)
    pre = jnp.dot(un_high, w_ref[...], preferred_element_type=F32) + bias_ref[...]
    pre = pre + jnp.dot(un_low, w_ref[...], preferred_element_type=F32)
    s = jax.nn.sigmoid(pre)
    grad = (cot_ref[...] * s * (1.0 + pre * (1.0 - s))).astype(BF16)
    own[...] = grad

    passed = list(started)
    started.clear()
    for d in near:
        go(own, band_ref.at[x, z], s_gz.at[d], r_gz.at[d], zdev(d))
    go(own, band_ref.at[x, z], s_gr.at[0], r_gl.at[0], xdev(right))
    go(own, band_ref.at[x, z], s_gl.at[0], r_gr.at[0], xdev(left))
    band_ref[x, z] = grad
    act_v[...] = pre * s
    act_out = pltpu.make_async_copy(act_v, act_ref, s_out.at[0])
    act_out.start()

    gw = jnp.dot(ut, grad, preferred_element_type=F32)
    wbuf[0:2] = gw.reshape(2, NZ, 8, T)
    gb = jnp.sum(grad.astype(F32), axis=0, keepdims=True)
    wbuf[2] = jnp.broadcast_to(gb.reshape(1, 1, T), (NZ, 8, T))
    wbuf[3] = jnp.zeros((NZ, 8, T), F32)

    half_a = (0, 7, 6, 5)

    def spread(d):
        zz = zfrom(d)
        arrived(band_ref.at[x, zz], s_gz.at[d], r_gz.at[d])
        go(band_ref.at[x, zz], band_ref.at[x, zz], s_gr.at[d], r_gl.at[d], xdev(right))
        go(band_ref.at[x, zz], band_ref.at[x, zz], s_gl.at[d], r_gr.at[d], xdev(left))

    def relay(d):
        zz = zfrom(d)
        arrived(band_ref.at[left, zz], s_gr.at[0], r_gl.at[d])
        if d in half_a:
            go(band_ref.at[left, zz], band_ref.at[left, zz], s_rel.at[d], r_rel.at[d], xdev(right))
        arrived(band_ref.at[right, zz], s_gr.at[0], r_gr.at[d])
        if d not in half_a:
            go(band_ref.at[right, zz], band_ref.at[right, zz], s_rel.at[d], r_rel.at[d], xdev(left))

    for copy in passed:
        copy.wait_send()
    for d in (1, 7, 2, 6):
        spread(d)
    relay(0)
    spread(3)
    relay(1)
    spread(5)
    relay(7)
    spread(4)
    for d in far:
        go(wbuf.at[:, zof(d)], wzin.at[d], s_wz.at[d], r_wz.at[d], zdev(d))
    for d in (2, 6, 3, 5, 4):
        relay(d)
    wsum = wbuf[:, z]
    for d in near:
        arrived(wzin.at[d], s_wz.at[d], r_wz.at[d])
        wsum = wsum + wzin[d]
    wx[...] = wsum
    for e in (2, 1, 3):
        xx = lax.rem(x + e, NX)
        go(wx.at[xx], wxin.at[e], s_wx.at[e], r_wx.at[e], xdev(xx))
    for d in (0,) + near:
        arrived(band_ref.at[across, zfrom(d)], s_rel.at[d], r_rel.at[d])

    def backward(g, carry):
        for u in range(STEP):
            t = g * STEP + u
            r = rows_ref[0, t]
            prod = jnp.dot(dense[t], band_ref[r // NZ, r % NZ], preferred_element_type=F32)
            prefix[t] = prefix[table[2, t]] + prod
        return carry

    steps = tiles // STEP
    lax.fori_loop(0, steps // 8, backward, 0)
    wtotal = wx[x]
    for e in (1, 3, 2):
        arrived(wxin.at[e], s_wx.at[e], r_wx.at[e])
        wtotal = wtotal + wxin[e]
    wcol[...] = wtotal
    go(wcol, wpin, s_wp, r_wp, partner)
    lax.fori_loop(steps // 8, steps * 3 // 8, backward, 0)
    arrived(wpin, s_wp, r_wp)
    wpair = wtotal + wpin[...]
    wp[...] = wpair
    for d in far:
        go(wp, wyin.at[d], s_wy.at[d], r_wy.at[d], ydev(d))
    lax.fori_loop(steps * 3 // 8, steps, backward, 0)

    contract = (((1,), (1,)), ((), ()))
    for c in range(fbuf.shape[3] // T):
        value = prefix[table[3, c]]
        high = value.astype(BF16)
        low = (value - high.astype(F32)).astype(BF16)
        term = lax.dot_general(w_ref[...], high, contract, preferred_element_type=F32)
        term += lax.dot_general(w_ref[...], low, contract, preferred_element_type=F32)
        fbuf[:, :, :, c * T : (c + 1) * T] = term.reshape(NY, NK, 8, T)

    passed = list(started)
    started.clear()
    for d in far + (0,):
        go(fbuf.at[yof(d), 1 - k], pin.at[d], s_p.at[d], r_p.at[d], partner)
    wtotal = wpair
    for d in near:
        arrived(wyin.at[d], s_wy.at[d], r_wy.at[d])
        wtotal = wtotal + wyin[d]
    wt[...] = wtotal
    wall[x, z] = wtotal
    for d in far:
        arrived(pin.at[d], s_p.at[d], r_p.at[d])
        sbuf[d] = (pin[d] + fbuf[yof(d), k]).astype(BF16)
        go(sbuf.at[d], yin.at[d], s_y.at[d], r_y.at[d], ydev(d))
        if d == 4:
            for dz in far:
                go(wt, wall.at[x, z], s_oz.at[dz], r_oz.at[dz], zdev(dz))
    arrived(pin.at[0], s_p.at[0], r_p.at[0])
    total = pin[0] + fbuf[y, k]
    for copy in passed:
        copy.wait_send()
    act_out.wait()
    for d in near:
        arrived(wall.at[x, zfrom(d)], s_oz.at[d], r_oz.at[d])
    for e in (2, 1, 3):
        go(wall.at[x], wall.at[x], s_ox.at[e], r_ox.at[e], xdev(lax.rem(x + e, NX)))
    for d in near:
        arrived(yin.at[d], s_y.at[d], r_y.at[d])
        total = total + yin[d].astype(F32)
    grad_v[...] = total.astype(BF16)
    grad_out = pltpu.make_async_copy(grad_v, grad_ref, s_out.at[1])
    grad_out.start()
    for e in (1, 3, 2):
        arrived(wall.at[lax.rem(x + NX - e, NX)], s_ox.at[e], r_ox.at[e])
    wall_out = pltpu.make_async_copy(wall, wout_ref, s_out.at[2])
    wall_out.start()
    drain()
    grad_out.wait()
    wall_out.wait()


def finish_kernel(shrink, act_ref, grad_ref, w_ref, act_out, grad_out, w_out, b_out):
    act_out[...] = act_ref[...]
    grad_out[...] = grad_ref[...]
    w_out[...] = w_ref[0:16].reshape(16 * 8, T) * shrink
    b_out[...] = w_ref[16][0:1, :] * shrink


def dma(*shape):
    return pltpu.SemaphoreType.DMA(shape)


def shards(features, weight, bias_vector, tile_rows, tile_cols, neighbours, edge_weights, tile_count, cotangent):
    nodes, width = features.shape
    hidden = weight.shape[1]
    tiles = neighbours.shape[2]
    shape = jax.ShapeDtypeStruct
    vbf = lambda *dims: pltpu.VMEM(dims, BF16)
    vf = lambda *dims: pltpu.VMEM(dims, F32)

    act, grad_t, wall = pl.pallas_call(
        whole_kernel,
        out_shape=(shape((T, hidden), F32), shape((width, nodes), BF16), shape((NX, NZ, 8, hidden), F32)),
        in_specs=[HBM_SPEC] * 9,
        out_specs=(HBM_SPEC,) * 3,
        scratch_shapes=[
            pltpu.SMEM((1, tiles), jnp.int32), pltpu.SMEM((1, tiles), jnp.int32), pltpu.SMEM((1, 1), jnp.int32),
            pltpu.VMEM((1, tiles), jnp.int32), pltpu.VMEM((1, tiles), jnp.int32),
            pltpu.VMEM(neighbours.shape[2:], jnp.int32), vbf(*edge_weights.shape[2:]),
            vbf(*weight.shape), vf(1, hidden), vf(T, hidden), dma(11),
            vbf(tiles, T, T), vf(tiles + 1, T, T), pltpu.VMEM((8, tiles), jnp.int32), pltpu.SMEM((8, tiles), jnp.int32),
            vbf(NY * NK, width, nodes), vbf(nodes // T, T, T), vbf(NX, NZ, T, T), vbf(NX, NZ, T, T),
            vf(NY, NK, width, nodes),
            vbf(4, T, T), vbf(4, T, T), vbf(4, T, T), vbf(4, T, T),
            vbf(NZ, T, T), vbf(NZ, T, T), vbf(NZ, T, T), vbf(NZ, T, T), vbf(T, T),
            vf(T, hidden), vbf(width, nodes), vf(NX, NZ, 8, T), dma(3),
            vf(NX, NZ, 8, T), vf(NX, 8, T), vf(NX, 8, T), vf(NZ, NX, 8, T),
            vf(8, T), vf(8, T), vf(8, T), vf(NY, 8, T), vf(8, T),
            vf(NY, width, nodes), vbf(NY, width, nodes), vbf(NY, width, nodes),
            dma(), dma(NY), dma(NY), dma(NY), dma(NY),
            dma(8), dma(8), dma(4), dma(4), dma(4), dma(4), dma(NZ), dma(NZ),
            dma(NZ), dma(NZ), dma(NZ), dma(NZ), dma(NZ), dma(NZ), dma(NZ), dma(NZ), dma(NZ), dma(NZ),
            dma(NX), dma(NX), dma(NZ), dma(NZ),
            dma(NY), dma(NY), dma(NY), dma(NY), dma(), dma(), dma(NY), dma(NY), dma(NZ), dma(NZ), dma(NX), dma(NX),
        ],
        compiler_params=pltpu.CompilerParams(collective_id=0, has_side_effects=True),
        name="whole",
    )(
        tile_rows[0], tile_cols[0], tile_count, features.T,
        neighbours[0, 0], edge_weights[0, 0], weight, bias_vector.reshape(1, hidden), cotangent,
    )

    node_count = cotangent.shape[0] * lax.axis_size("row") * lax.axis_size("col")
    shrink = float(node_count) ** (-0.5)
    act, grad_t, wgrad, bgrad = pl.pallas_call(
        functools.partial(finish_kernel, shrink),
        out_shape=(
            shape((T, hidden), F32), shape((width, nodes), BF16), shape((T, hidden), F32), shape((1, hidden), F32),
        ),
        in_specs=[VMEM_SPEC] * 3,
        out_specs=(VMEM_SPEC,) * 4,
        name="finish",
    )(act, grad_t, wall.reshape(NX * NZ, 8, hidden))
    return act, grad_t.T, wgrad, bgrad.reshape(hidden)


def solution(mesh):
    in_specs = (
        P("col", "row"),
        P(),
        P(),
        P("row", "col", None),
        P("row", "col", None),
        P("row", "col", None, None, None),
        P("row", "col", None, None, None),
        P("row", "col"),
        P(("row", "col"), None),
    )
    out_specs = (P(("row", "col"), None), P("col", "row"), P(), P())
    return jax.shard_map(shards, mesh=mesh, in_specs=in_specs, out_specs=out_specs, check_vma=False)
```

```python
import functools

import jax
import jax.numpy as jnp
from jax import lax
from jax.experimental import pallas as pl
from jax.experimental.pallas import tpu as pltpu
from jax.sharding import PartitionSpec as P

NX = 4
NZ = 8
NY = 8
NK = 2
T = 128
ONWARD = {2: ((2, 4), (1, 3)), 6: ((7, 5),)}
HALF = 64
STEP = 8
PARTS = ((0, 1, 7, 2), (6, 3, 5, 4))
ORDER = (4, 3, 2, 1, 5, 6, 7, 0)
F32 = jnp.float32
BF16 = jnp.bfloat16
MESH = pl.DeviceIdType.MESH
VMEM_SPEC = pl.BlockSpec(memory_space=pltpu.VMEM)
HBM_SPEC = pl.BlockSpec(memory_space=pltpu.HBM)


def place():
    row = lax.axis_index("row")
    col = lax.axis_index("col")
    return row, col, row // NK, row % NK, col // NZ, col % NZ


def remote(src, dst, send_sem, recv_sem, peer):
    return pltpu.make_async_remote_copy(
        src_ref=src,
        dst_ref=dst,
        send_sem=send_sem,
        recv_sem=recv_sem,
        device_id=peer,
        device_id_type=MESH,
    )


def tile_matrix(t, live, nb_ref, ew_ref, rows_iota):
    ids = nb_ref[t]
    values = ew_ref[t].astype(F32)
    values = jnp.where(live, values, jnp.zeros_like(values))
    second = jnp.where(rows_iota == ids[1:2, :], values[1:2, :], 0.0)
    return jnp.where(rows_iota == ids[0:1, :], values[0:1, :], second).astype(BF16)


def links(blocks_row, tiles):
    across = jnp.broadcast_to(blocks_row, (tiles, tiles))
    down = across.T
    first = lax.broadcasted_iota(jnp.int32, (tiles, tiles), 0)
    second = lax.broadcasted_iota(jnp.int32, (tiles, tiles), 1)
    before = jnp.max(jnp.where((down == across) & (first < second), first, -1), axis=0, keepdims=True)
    last = jnp.max(jnp.where(down == second, first, -1), axis=0, keepdims=True)
    pick = lambda v: jnp.minimum(jnp.where(v < 0, tiles, v), tiles)
    return pick(before), pick(last)


def whole_kernel(
    rows_hbm, cols_hbm, count_hbm, ft_hbm, nb_hbm, ew_hbm, w_hbm, bias_hbm, cot_hbm,
    act_ref, grad_ref, wout_ref,
    rows_ref, cols_ref, count_ref, rows_vec, cols_vec, nb_ref, ew_ref, w_ref, bias_ref, cot_ref, s_in,
    w_wide, w_turned, dense, prefix, table_v, table, ftraw, panel, u_ref, band_ref, fbuf,
    from_l_relay, from_r_relay, to_r, to_l, in_l, in_r, summed, zin, own,
    act_v, grad_v, wall, s_out, wbuf, wxin, wx, wzin, wcol, wpin, wp, wyin, wt,
    pin, sbuf, yin,
    s_tab, s_fy, r_fy, s_fp, r_fp,
    s_raw_r, s_raw_l, s_mix_r, s_mix_l, r_relay_l, r_relay_r, r_in_l, r_in_r,
    s_z, r_z, s_gz, r_gz, s_gr, s_gl, r_gl, r_gr, s_rel, r_rel, s_wx, r_wx, s_wz, r_wz,
    s_p, r_p, s_y, r_y, s_wp, r_wp, s_wy, r_wy, s_oz, r_oz, s_ox, r_ox,
):
    row, col, y, k, x, z = place()
    tiles = nb_ref.shape[0]
    right = lax.rem(x + 1, NX)
    left = lax.rem(x + NX - 1, NX)
    across = lax.rem(x + 2, NX)
    xdev = lambda xx: (row, xx * NZ + z)
    zof = lambda d: lax.rem(z + d, NZ)
    zfrom = lambda d: lax.rem(z + NZ - d, NZ)
    zdev = lambda d: (row, x * NZ + zof(d))
    partner = (y * NK + 1 - k, col)
    yof = lambda d: lax.rem(y + d, NY)
    ydev = lambda d: (yof(d) * NK + k, col)
    far = (4, 3, 5, 2, 6, 1, 7)
    near = (1, 7, 2, 6, 3, 5, 4)
    peers = [partner] + [ydev(d) for d in range(1, NY)]
    peers += [xdev(right), xdev(left), xdev(across)] + [zdev(d) for d in range(1, NZ)]

    def go(src, dst, send_sem, recv_sem, peer):
        remote(src, dst, send_sem, recv_sem, peer).start()

    def arrived(dst, send_sem, recv_sem):
        remote(dst, dst, send_sem, recv_sem, partner).wait_recv()

    def sent(like, send_sem):
        remote(like, like, send_sem, send_sem, partner).wait_send()

    barrier = pltpu.get_barrier_semaphore()
    for peer in peers:
        pl.semaphore_signal(barrier, inc=1, device_id=peer, device_id_type=MESH)

    pairs = (
        (rows_hbm, rows_vec), (cols_hbm, cols_vec), (nb_hbm, nb_ref), (ew_hbm, ew_ref), (count_hbm, count_ref),
        (ft_hbm, ftraw.at[row]), (rows_hbm, rows_ref), (cols_hbm, cols_ref), (w_hbm, w_ref), (bias_hbm, bias_ref),
        (cot_hbm, cot_ref),
    )
    loads = [pltpu.make_async_copy(src, dst, s_in.at[n]) for n, (src, dst) in enumerate(pairs)]
    for load in loads:
        load.start()
    loads[0].wait()
    loads[1].wait()
    row_before, row_last = links(rows_vec[...], tiles)
    col_before, col_last = links(cols_vec[...], tiles)
    table_v[0:1, :] = row_before
    table_v[1:2, :] = row_last
    table_v[2:3, :] = col_before
    table_v[3:4, :] = col_last
    table_v[4:8, :] = jnp.zeros((4, tiles), jnp.int32)
    to_smem = pltpu.make_async_copy(table_v, table, s_tab)
    to_smem.start()
    for load in loads[2:]:
        load.wait()
    count = count_ref[0, 0]
    iota = lax.broadcasted_iota(jnp.int32, (T, T), 0)

    def build(g, carry):
        for u in range(4):
            t = g * 4 + u
            dense[t] = tile_matrix(t, t < count, nb_ref, ew_ref, iota)
        return carry

    lax.fori_loop(0, tiles // 4, build, 0)
    prefix[tiles] = jnp.zeros((T, T), F32)
    pl.semaphore_wait(barrier, len(peers))

    for d in (2, 6, 1, 7):
        go(ftraw.at[row], ftraw.at[row], s_fy, r_fy.at[d], ydev(d))
    go(ftraw.at[row], ftraw.at[row], s_fp, r_fp.at[0], partner)
    to_smem.wait()
    ysource = lambda d: lax.rem(y + NY - d, NY)

    def pass_on(d):
        slot = ysource(d) * NK + k
        arrived(ftraw.at[slot], s_fy, r_fy.at[d])
        for step, there in ONWARD.get(d, ()):
            go(ftraw.at[slot], ftraw.at[slot], s_fy, r_fy.at[there], ydev(step))
        go(ftraw.at[slot], ftraw.at[slot], s_fp, r_fp.at[d], partner)

    def fill_panel(h):
        for d in PARTS[h]:
            arrived(ftraw.at[ysource(d) * NK + 1 - k], s_fp, r_fp.at[d])
        for c in range(NX * NZ // 2):
            pieces = [ftraw[pl.ds(ysource(d) * NK, NK), :, c * T : (c + 1) * T] for d in PARTS[h]]
            wide = jnp.concatenate([p.astype(F32).reshape(2 * 8, T) for p in pieces], axis=0)
            panel[h, c] = wide.astype(BF16)

    w_wide[...] = w_ref[...].astype(F32).reshape(NY * NK, 8, T)
    pieces = [w_wide[pl.ds(ysource(d) * NK, NK)].reshape(2 * 8, T) for d in PARTS[0] + PARTS[1]]
    w_turned[...] = jnp.concatenate(pieces, axis=0).astype(BF16)

    def forward(h):
        low, high = h * HALF, (h + 1) * HALF

        def steps(g, carry):
            for u in range(STEP):
                t = g * STEP + u
                prod = jnp.dot(panel[h, cols_ref[0, t]], dense[t], preferred_element_type=F32)
                prefix[t, low:high] = prefix[table[0, t], low:high] + prod
            return carry

        return steps

    def block_row(h, xx, p):
        block = xx * NZ + zof(ORDER[p])
        u_ref[h, xx, p] = prefix[table[1, block], h * HALF : (h + 1) * HALF].astype(BF16)

    def sums_start(h):
        for p in range(NZ):
            block_row(h, across, p)
        for q in (0, 2):
            go(u_ref.at[h, across, q : q + 2], from_l_relay.at[h, q : q + 2], s_raw_r.at[h], r_relay_l.at[h, q], xdev(right))
            go(u_ref.at[h, across, 4 + q : 6 + q], from_r_relay.at[h, q : q + 2], s_raw_l.at[h], r_relay_r.at[h, q], xdev(left))
        for p in range(NZ):
            block_row(h, right, p)
            block_row(h, left, p)
            block_row(h, x, p)

    def sums_relay(h):
        for q in (0, 2):
            a, b = slice(q, q + 2), slice(4 + q, 6 + q)
            arrived(from_l_relay.at[h, a], s_raw_r.at[h], r_relay_l.at[h, q])
            to_r[h, a] = (from_l_relay[h, a].astype(F32) + u_ref[h, right, a].astype(F32)).astype(BF16)
            arrived(from_r_relay.at[h, a], s_raw_l.at[h], r_relay_r.at[h, q])
            to_l[h, a] = (from_r_relay[h, a].astype(F32) + u_ref[h, left, b].astype(F32)).astype(BF16)
            go(to_r.at[h, a], in_l.at[h, a], s_mix_r.at[h], r_in_l.at[h, q], xdev(right))
            go(to_l.at[h, a], in_r.at[h, b], s_mix_l.at[h], r_in_r.at[h, 4 + q], xdev(left))
            go(u_ref.at[h, right, b], in_l.at[h, b], s_raw_r.at[h], r_in_l.at[h, 4 + q], xdev(right))
            go(u_ref.at[h, left, a], in_r.at[h, a], s_raw_l.at[h], r_in_r.at[h, q], xdev(left))

    def xsum(h, p):
        return u_ref[h, x, p].astype(F32) + in_l[h, p].astype(F32) + in_r[h, p].astype(F32)

    def sums_z(h):
        own_part = None
        for q in (0, 4, 2, 6):
            pair = slice(q, q + 2)
            arrived(in_l.at[h, pair], s_raw_r.at[h], r_in_l.at[h, q])
            arrived(in_r.at[h, pair], s_raw_r.at[h], r_in_r.at[h, q])
            for p in (q, q + 1):
                d = ORDER[p]
                if d == 0:
                    own_part = xsum(h, p)
                else:
                    summed[h, d] = xsum(h, p).astype(BF16)
            for p in (q, q + 1):
                d = ORDER[p]
                if d:
                    go(summed.at[h, d], zin.at[h, d], s_z.at[h], r_z.at[h, d], zdev(d))
        return own_part

    def sums_end(h, value):
        for d in near:
            arrived(zin.at[h, d], s_z.at[h], r_z.at[h, d])
            value = value + zin[h, d].astype(F32)
        return value

    def sums_sent(h):
        sent(u_ref.at[h, 0], s_raw_r.at[h])
        sent(u_ref.at[h, 0], s_raw_l.at[h])
        sent(to_r.at[h], s_mix_r.at[h])
        sent(to_l.at[h], s_mix_l.at[h])
        sent(summed.at[h, 1:NZ], s_z.at[h])

    steps = tiles // STEP
    for d in (2, 6, 1, 7):
        pass_on(d)
    fill_panel(0)
    lax.fori_loop(0, steps // 2, forward(0), 0)
    for d in (3, 5):
        pass_on(d)
    lax.fori_loop(steps // 2, steps, forward(0), 0)
    pass_on(4)
    sums_start(0)
    fill_panel(1)
    lax.fori_loop(0, steps // 2, forward(1), 0)
    sums_relay(0)
    lax.fori_loop(steps // 2, steps, forward(1), 0)
    sums_start(1)
    first = sums_z(0)
    sums_relay(1)
    second = sums_z(1)
    total = jnp.concatenate([sums_end(0, first), sums_end(1, second)], axis=0)

    ut = total.astype(BF16)
    un = total.T
    un_high = un.astype(BF16)
    un_low = (un - un_high.astype(F32)).astype(BF16)
    pre = jnp.dot(un_high, w_turned[...], preferred_element_type=F32) + bias_ref[...]
    pre = pre + jnp.dot(un_low, w_turned[...], preferred_element_type=F32)
    s = jax.nn.sigmoid(pre)
    grad = (cot_ref[...] * s * (1.0 + pre * (1.0 - s))).astype(BF16)
    own[...] = grad

    for d in near:
        go(own, band_ref.at[x, z], s_gz, r_gz.at[d], zdev(d))
    go(own, band_ref.at[x, z], s_gr, r_gl.at[0], xdev(right))
    go(own, band_ref.at[x, z], s_gl, r_gr.at[0], xdev(left))
    band_ref[x, z] = grad
    act_v[...] = pre * s
    act_out = pltpu.make_async_copy(act_v, act_ref, s_out.at[0])
    act_out.start()

    gw = jnp.dot(ut, grad, preferred_element_type=F32)
    for n, d in enumerate(PARTS[0] + PARTS[1]):
        for kk in range(NK):
            slot = ysource(d) * NK + kk
            at = (n * NK + kk) * 8
            wbuf[slot // NZ, slot % NZ] = gw[at : at + 8]
    gb = jnp.sum(grad.astype(F32), axis=0, keepdims=True)
    wbuf[2] = jnp.broadcast_to(gb.reshape(1, 1, T), (NZ, 8, T))
    wbuf[3] = jnp.zeros((NZ, 8, T), F32)

    half_a = (0, 7, 6, 5)

    def spread(d):
        zz = zfrom(d)
        arrived(band_ref.at[x, zz], s_gz, r_gz.at[d])
        go(band_ref.at[x, zz], band_ref.at[x, zz], s_gr, r_gl.at[d], xdev(right))
        go(band_ref.at[x, zz], band_ref.at[x, zz], s_gl, r_gr.at[d], xdev(left))

    def relay(d):
        zz = zfrom(d)
        arrived(band_ref.at[left, zz], s_gr, r_gl.at[d])
        if d in half_a:
            go(band_ref.at[left, zz], band_ref.at[left, zz], s_rel, r_rel.at[d], xdev(right))
        arrived(band_ref.at[right, zz], s_gr, r_gr.at[d])
        if d not in half_a:
            go(band_ref.at[right, zz], band_ref.at[right, zz], s_rel, r_rel.at[d], xdev(left))

    sent(ftraw.at[0 : NY - 1], s_fy)
    sent(ftraw.at[0:NY], s_fp)
    sums_sent(0)
    sums_sent(1)
    for d in (1, 7, 2, 6):
        spread(d)
    relay(0)
    spread(3)
    relay(1)
    spread(5)
    relay(7)
    spread(4)
    for d in far:
        go(wbuf.at[:, zof(d)], wzin.at[d], s_wz, r_wz.at[d], zdev(d))
    for d in (2, 6, 3, 5, 4):
        relay(d)
    wsum = wbuf[:, z]
    for d in near:
        arrived(wzin.at[d], s_wz, r_wz.at[d])
        wsum = wsum + wzin[d]
    wx[...] = wsum
    for e in (2, 1, 3):
        xx = lax.rem(x + e, NX)
        go(wx.at[xx], wxin.at[e], s_wx, r_wx.at[e], xdev(xx))
    for d in (0,) + near:
        arrived(band_ref.at[across, zfrom(d)], s_rel, r_rel.at[d])

    def backward(g, carry):
        for u in range(STEP):
            t = g * STEP + u
            r = rows_ref[0, t]
            prod = jnp.dot(dense[t], band_ref[r // NZ, r % NZ], preferred_element_type=F32)
            prefix[t] = prefix[table[2, t]] + prod
        return carry

    lax.fori_loop(0, steps // 8, backward, 0)
    wtotal = wx[x]
    for e in (1, 3, 2):
        arrived(wxin.at[e], s_wx, r_wx.at[e])
        wtotal = wtotal + wxin[e]
    wcol[...] = wtotal
    go(wcol, wpin, s_wp, r_wp, partner)
    lax.fori_loop(steps // 8, steps * 3 // 8, backward, 0)
    arrived(wpin, s_wp, r_wp)
    wpair = wtotal + wpin[...]
    wp[...] = wpair
    for d in far:
        go(wp, wyin.at[d], s_wy, r_wy.at[d], ydev(d))
    lax.fori_loop(steps * 3 // 8, steps, backward, 0)

    contract = (((1,), (1,)), ((), ()))
    for c in range(fbuf.shape[3] // T):
        value = prefix[table[3, c]]
        high = value.astype(BF16)
        low = (value - high.astype(F32)).astype(BF16)
        term = lax.dot_general(w_ref[...], high, contract, preferred_element_type=F32)
        term += lax.dot_general(w_ref[...], low, contract, preferred_element_type=F32)
        fbuf[:, :, :, c * T : (c + 1) * T] = term.reshape(NY, NK, 8, T)

    for d in far + (0,):
        go(fbuf.at[yof(d), 1 - k], pin.at[d], s_p, r_p.at[d], partner)
    wtotal = wpair
    for d in near:
        arrived(wyin.at[d], s_wy, r_wy.at[d])
        wtotal = wtotal + wyin[d]
    wt[...] = wtotal
    wall[x, z] = wtotal
    for d in far:
        arrived(pin.at[d], s_p, r_p.at[d])
        sbuf[d] = (pin[d] + fbuf[yof(d), k]).astype(BF16)
        go(sbuf.at[d], yin.at[d], s_y, r_y.at[d], ydev(d))
        if d == 4:
            for dz in far:
                go(wt, wall.at[x, z], s_oz, r_oz.at[dz], zdev(dz))
    arrived(pin.at[0], s_p, r_p.at[0])
    total = pin[0] + fbuf[y, k]
    sent(band_ref.at[0, 0 : NZ - 1], s_gz)
    for sem in (s_gr, s_gl, s_rel):
        sent(band_ref.at[0], sem)
    sent(wzin.at[1:NZ], s_wz)
    sent(wxin.at[1:NX], s_wx)
    sent(wpin, s_wp)
    sent(wyin.at[1:NY], s_wy)
    act_out.wait()
    for d in near:
        arrived(wall.at[x, zfrom(d)], s_oz, r_oz.at[d])
    for e in (2, 1, 3):
        go(wall.at[x], wall.at[x], s_ox, r_ox.at[e], xdev(lax.rem(x + e, NX)))
    for d in near:
        arrived(yin.at[d], s_y, r_y.at[d])
        total = total + yin[d].astype(F32)
    grad_v[...] = total.astype(BF16)
    grad_out = pltpu.make_async_copy(grad_v, grad_ref, s_out.at[1])
    grad_out.start()
    for e in (1, 3, 2):
        arrived(wall.at[lax.rem(x + NX - e, NX)], s_ox, r_ox.at[e])
    wall_out = pltpu.make_async_copy(wall, wout_ref, s_out.at[2])
    wall_out.start()
    sent(pin, s_p)
    sent(yin.at[1:NY], s_y)
    sent(wyin.at[1:NZ], s_oz)
    sent(wall.at[1:NX], s_ox)
    grad_out.wait()
    wall_out.wait()


def finish_kernel(shrink, act_ref, grad_ref, w_ref, act_out, grad_out, w_out, b_out):
    act_out[...] = act_ref[...]
    grad_out[...] = grad_ref[...]
    w_out[...] = w_ref[0:16].reshape(16 * 8, T) * shrink
    b_out[...] = w_ref[16][0:1, :] * shrink


def dma(*shape):
    return pltpu.SemaphoreType.DMA(shape)


def shards(features, weight, bias_vector, tile_rows, tile_cols, neighbours, edge_weights, tile_count, cotangent):
    nodes, width = features.shape
    hidden = weight.shape[1]
    tiles = neighbours.shape[2]
    shape = jax.ShapeDtypeStruct
    vbf = lambda *dims: pltpu.VMEM(dims, BF16)
    vf = lambda *dims: pltpu.VMEM(dims, F32)

    act, grad_t, wall = pl.pallas_call(
        whole_kernel,
        out_shape=(shape((T, hidden), F32), shape((width, nodes), BF16), shape((NX, NZ, 8, hidden), F32)),
        in_specs=[HBM_SPEC] * 9,
        out_specs=(HBM_SPEC,) * 3,
        scratch_shapes=[
            pltpu.SMEM((1, tiles), jnp.int32), pltpu.SMEM((1, tiles), jnp.int32), pltpu.SMEM((1, 1), jnp.int32),
            pltpu.VMEM((1, tiles), jnp.int32), pltpu.VMEM((1, tiles), jnp.int32),
            pltpu.VMEM(neighbours.shape[2:], jnp.int32), vbf(*edge_weights.shape[2:]),
            vbf(*weight.shape), vf(1, hidden), vf(T, hidden), dma(11),
            vf(NY * NK, 8, hidden), vbf(T, hidden), vbf(tiles, T, T), vf(tiles + 1, T, T), pltpu.VMEM((8, tiles), jnp.int32), pltpu.SMEM((8, tiles), jnp.int32),
            vbf(NY * NK, width, nodes), vbf(2, nodes // T, HALF, T), vbf(2, NX, NZ, HALF, T), vbf(NX, NZ, T, T),
            vf(NY, NK, width, nodes),
            vbf(2, 4, HALF, T), vbf(2, 4, HALF, T), vbf(2, 4, HALF, T), vbf(2, 4, HALF, T),
            vbf(2, NZ, HALF, T), vbf(2, NZ, HALF, T), vbf(2, NZ, HALF, T), vbf(2, NZ, HALF, T), vbf(T, T),
            vf(T, hidden), vbf(width, nodes), vf(NX, NZ, 8, T), dma(3),
            vf(NX, NZ, 8, T), vf(NX, 8, T), vf(NX, 8, T), vf(NZ, NX, 8, T),
            vf(8, T), vf(8, T), vf(8, T), vf(NY, 8, T), vf(8, T),
            vf(NY, width, nodes), vbf(NY, width, nodes), vbf(NY, width, nodes),
            dma(), dma(), dma(NY), dma(), dma(NY),
            dma(2), dma(2), dma(2), dma(2), dma(2, 4), dma(2, 4), dma(2, NZ), dma(2, NZ),
            dma(2), dma(2, NZ), dma(), dma(NZ), dma(), dma(), dma(NZ), dma(NZ), dma(), dma(NZ),
            dma(), dma(NX), dma(), dma(NZ),
            dma(), dma(NY), dma(), dma(NY), dma(), dma(), dma(), dma(NY), dma(), dma(NZ), dma(), dma(NX),
        ],
        compiler_params=pltpu.CompilerParams(collective_id=0, has_side_effects=True),
        name="whole",
    )(
        tile_rows[0], tile_cols[0], tile_count, features.T,
        neighbours[0, 0], edge_weights[0, 0], weight, bias_vector.reshape(1, hidden), cotangent,
    )

    node_count = cotangent.shape[0] * lax.axis_size("row") * lax.axis_size("col")
    shrink = float(node_count) ** (-0.5)
    act, grad_t, wgrad, bgrad = pl.pallas_call(
        functools.partial(finish_kernel, shrink),
        out_shape=(
            shape((T, hidden), F32), shape((width, nodes), BF16), shape((T, hidden), F32), shape((1, hidden), F32),
        ),
        in_specs=[VMEM_SPEC] * 3,
        out_specs=(VMEM_SPEC,) * 4,
        name="finish",
    )(act, grad_t, wall.reshape(NX * NZ, 8, hidden))
    return act, grad_t.T, wgrad, bgrad.reshape(hidden)


def solution(mesh):
    in_specs = (
        P("col", "row"),
        P(),
        P(),
        P("row", "col", None),
        P("row", "col", None),
        P("row", "col", None, None, None),
        P("row", "col", None, None, None),
        P("row", "col"),
        P(("row", "col"), None),
    )
    out_specs = (P(("row", "col"), None), P("col", "row"), P(), P())
    return jax.shard_map(shards, mesh=mesh, in_specs=in_specs, out_specs=out_specs, check_vma=False)
```

```python
import functools

import jax
import jax.numpy as jnp
from jax import lax
from jax.experimental import pallas as pl
from jax.experimental.pallas import tpu as pltpu
from jax.sharding import PartitionSpec as P

NX = 4
NZ = 8
NY = 8
NK = 2
T = 128
ONWARD = {2: ((2, 4), (1, 3)), 6: ((7, 5),)}
HALF = 64
STEP = 8
PARTS = ((0, 1, 7, 2), (6, 3, 5, 4))
ORDER = (4, 3, 2, 1, 5, 6, 7, 0)
F32 = jnp.float32
BF16 = jnp.bfloat16
MESH = pl.DeviceIdType.MESH
VMEM_SPEC = pl.BlockSpec(memory_space=pltpu.VMEM)
HBM_SPEC = pl.BlockSpec(memory_space=pltpu.HBM)


def place():
    row = lax.axis_index("row")
    col = lax.axis_index("col")
    return row, col, row // NK, row % NK, col // NZ, col % NZ


def remote(src, dst, send_sem, recv_sem, peer):
    return pltpu.make_async_remote_copy(
        src_ref=src,
        dst_ref=dst,
        send_sem=send_sem,
        recv_sem=recv_sem,
        device_id=peer,
        device_id_type=MESH,
    )


def tile_matrix(t, live, nb_ref, ew_ref, rows_iota):
    ids = nb_ref[t]
    values = ew_ref[t].astype(F32)
    values = jnp.where(live, values, jnp.zeros_like(values))
    second = jnp.where(rows_iota == ids[1:2, :], values[1:2, :], 0.0)
    return jnp.where(rows_iota == ids[0:1, :], values[0:1, :], second).astype(BF16)


def links(blocks_row, tiles):
    across = jnp.broadcast_to(blocks_row, (tiles, tiles))
    down = across.T
    first = lax.broadcasted_iota(jnp.int32, (tiles, tiles), 0)
    second = lax.broadcasted_iota(jnp.int32, (tiles, tiles), 1)
    before = jnp.max(jnp.where((down == across) & (first < second), first, -1), axis=0, keepdims=True)
    last = jnp.max(jnp.where(down == second, first, -1), axis=0, keepdims=True)
    pick = lambda v: jnp.minimum(jnp.where(v < 0, tiles, v), tiles)
    return pick(before), pick(last)


def whole_kernel(
    rows_hbm, cols_hbm, count_hbm, ft_hbm, nb_hbm, ew_hbm, w_hbm, bias_hbm, cot_hbm,
    act_ref, grad_ref, wout_ref,
    rows_ref, cols_ref, count_ref, rows_vec, cols_vec, nb_ref, ew_ref, w_ref, bias_ref, cot_ref, s_in,
    w_wide, w_turned, dense, prefix, table_v, table, ftraw, panel, u_ref, band_ref, fbuf,
    from_l_relay, from_r_relay, to_r, to_l, in_l, in_r, summed, zin, own,
    act_v, grad_v, wall, s_out, wbuf, wxin, wx, wzin, wcol, wpin, wp, wyin, wt,
    pin, sbuf, yin,
    s_tab, s_fy, r_fy, s_fp, r_fp,
    s_raw_r, s_raw_l, s_mix_r, s_mix_l, r_relay_l, r_relay_r, r_in_l, r_in_r,
    s_z, r_z, s_gz, r_gz, s_gr, s_gl, r_gl, r_gr, s_rel, r_rel, s_wx, r_wx, s_wz, r_wz,
    s_p, r_p, s_y, r_y, s_wp, r_wp, s_wy, r_wy, s_oz, r_oz, s_ox, r_ox,
):
    row, col, y, k, x, z = place()
    tiles = nb_ref.shape[0]
    right = lax.rem(x + 1, NX)
    left = lax.rem(x + NX - 1, NX)
    across = lax.rem(x + 2, NX)
    xdev = lambda xx: (row, xx * NZ + z)
    zof = lambda d: lax.rem(z + d, NZ)
    zfrom = lambda d: lax.rem(z + NZ - d, NZ)
    zdev = lambda d: (row, x * NZ + zof(d))
    partner = (y * NK + 1 - k, col)
    yof = lambda d: lax.rem(y + d, NY)
    ydev = lambda d: (yof(d) * NK + k, col)
    far = (4, 3, 5, 2, 6, 1, 7)
    near = (1, 7, 2, 6, 3, 5, 4)
    peers = [partner] + [ydev(d) for d in range(1, NY)]
    peers += [xdev(right), xdev(left), xdev(across)] + [zdev(d) for d in range(1, NZ)]

    def go(src, dst, send_sem, recv_sem, peer):
        remote(src, dst, send_sem, recv_sem, peer).start()

    def arrived(dst, send_sem, recv_sem):
        remote(dst, dst, send_sem, recv_sem, partner).wait_recv()

    def sent(like, send_sem):
        remote(like, like, send_sem, send_sem, partner).wait_send()

    barrier = pltpu.get_barrier_semaphore()
    for peer in peers:
        pl.semaphore_signal(barrier, inc=1, device_id=peer, device_id_type=MESH)

    pairs = (
        (rows_hbm, rows_vec), (cols_hbm, cols_vec), (nb_hbm, nb_ref), (ew_hbm, ew_ref), (count_hbm, count_ref),
        (ft_hbm, ftraw.at[row]), (rows_hbm, rows_ref), (cols_hbm, cols_ref), (w_hbm, w_ref), (bias_hbm, bias_ref),
        (cot_hbm, cot_ref),
    )
    loads = [pltpu.make_async_copy(src, dst, s_in.at[n]) for n, (src, dst) in enumerate(pairs)]
    for load in loads:
        load.start()
    loads[0].wait()
    loads[1].wait()
    row_before, row_last = links(rows_vec[...], tiles)
    col_before, col_last = links(cols_vec[...], tiles)
    table_v[0:1, :] = row_before
    table_v[1:2, :] = row_last
    table_v[2:3, :] = col_before
    table_v[3:4, :] = col_last
    table_v[4:8, :] = jnp.zeros((4, tiles), jnp.int32)
    to_smem = pltpu.make_async_copy(table_v, table, s_tab)
    to_smem.start()
    for load in loads[2:]:
        load.wait()
    count = count_ref[0, 0]
    iota = lax.broadcasted_iota(jnp.int32, (T, T), 0)

    def build(g, carry):
        for u in range(4):
            t = g * 4 + u
            dense[t] = tile_matrix(t, t < count, nb_ref, ew_ref, iota)
        return carry

    lax.fori_loop(0, tiles // 4, build, 0)
    prefix[tiles] = jnp.zeros((T, T), F32)
    pl.semaphore_wait(barrier, len(peers))

    for d in (2, 6, 1, 7):
        go(ftraw.at[row], ftraw.at[row], s_fy, r_fy.at[d], ydev(d))
    go(ftraw.at[row], ftraw.at[row], s_fp, r_fp.at[0], partner)
    to_smem.wait()
    ysource = lambda d: lax.rem(y + NY - d, NY)

    def pass_on(d):
        slot = ysource(d) * NK + k
        arrived(ftraw.at[slot], s_fy, r_fy.at[d])
        for step, there in ONWARD.get(d, ()):
            go(ftraw.at[slot], ftraw.at[slot], s_fy, r_fy.at[there], ydev(step))
        go(ftraw.at[slot], ftraw.at[slot], s_fp, r_fp.at[d], partner)

    def fill_panel(h):
        for d in PARTS[h]:
            arrived(ftraw.at[ysource(d) * NK + 1 - k], s_fp, r_fp.at[d])
        for c in range(NX * NZ // 2):
            pieces = [ftraw[pl.ds(ysource(d) * NK, NK), :, c * T : (c + 1) * T] for d in PARTS[h]]
            wide = jnp.concatenate([p.astype(F32).reshape(2 * 8, T) for p in pieces], axis=0)
            panel[h, c] = wide.astype(BF16)

    w_wide[...] = w_ref[...].astype(F32).reshape(NY * NK, 8, T)
    pieces = [w_wide[pl.ds(ysource(d) * NK, NK)].reshape(2 * 8, T) for d in PARTS[0] + PARTS[1]]
    w_turned[...] = jnp.concatenate(pieces, axis=0).astype(BF16)

    def forward(h):
        low, high = h * HALF, (h + 1) * HALF

        def steps(g, carry):
            for u in range(STEP):
                t = g * STEP + u
                prod = jnp.dot(panel[h, cols_ref[0, t]], dense[t], preferred_element_type=F32)
                prefix[t, low:high] = prefix[table[0, t], low:high] + prod
            return carry

        return steps

    def block_row(h, xx, p):
        block = xx * NZ + zof(ORDER[p])
        u_ref[h, xx, p] = prefix[table[1, block], h * HALF : (h + 1) * HALF].astype(BF16)

    def sums_start(h):
        for p in range(NZ):
            block_row(h, across, p)
        for q in (0, 2):
            go(u_ref.at[h, across, q : q + 2], from_l_relay.at[h, q : q + 2], s_raw_r.at[h], r_relay_l.at[h, q], xdev(right))
            go(u_ref.at[h, across, 4 + q : 6 + q], from_r_relay.at[h, q : q + 2], s_raw_l.at[h], r_relay_r.at[h, q], xdev(left))
        for p in range(NZ):
            block_row(h, right, p)
            block_row(h, left, p)
            block_row(h, x, p)

    def sums_relay(h, pairs=(0, 2)):
        for q in pairs:
            a, b = slice(q, q + 2), slice(4 + q, 6 + q)
            arrived(from_l_relay.at[h, a], s_raw_r.at[h], r_relay_l.at[h, q])
            to_r[h, a] = (from_l_relay[h, a].astype(F32) + u_ref[h, right, a].astype(F32)).astype(BF16)
            arrived(from_r_relay.at[h, a], s_raw_l.at[h], r_relay_r.at[h, q])
            to_l[h, a] = (from_r_relay[h, a].astype(F32) + u_ref[h, left, b].astype(F32)).astype(BF16)
            go(to_r.at[h, a], in_l.at[h, a], s_mix_r.at[h], r_in_l.at[h, q], xdev(right))
            go(to_l.at[h, a], in_r.at[h, b], s_mix_l.at[h], r_in_r.at[h, 4 + q], xdev(left))
            go(u_ref.at[h, right, b], in_l.at[h, b], s_raw_r.at[h], r_in_l.at[h, 4 + q], xdev(right))
            go(u_ref.at[h, left, a], in_r.at[h, a], s_raw_l.at[h], r_in_r.at[h, q], xdev(left))

    def xsum(h, p):
        return u_ref[h, x, p].astype(F32) + in_l[h, p].astype(F32) + in_r[h, p].astype(F32)

    def sums_z(h):
        own_part = None
        for q in (0, 4, 2, 6):
            pair = slice(q, q + 2)
            arrived(in_l.at[h, pair], s_raw_r.at[h], r_in_l.at[h, q])
            arrived(in_r.at[h, pair], s_raw_r.at[h], r_in_r.at[h, q])
            for p in (q, q + 1):
                d = ORDER[p]
                if d == 0:
                    own_part = xsum(h, p)
                else:
                    summed[h, d] = xsum(h, p).astype(BF16)
            for p in (q, q + 1):
                d = ORDER[p]
                if d:
                    go(summed.at[h, d], zin.at[h, d], s_z.at[h], r_z.at[h, d], zdev(d))
        return own_part

    def sums_end(h, value):
        for d in near:
            arrived(zin.at[h, d], s_z.at[h], r_z.at[h, d])
            value = value + zin[h, d].astype(F32)
        return value

    def sums_sent(h):
        sent(u_ref.at[h, 0], s_raw_r.at[h])
        sent(u_ref.at[h, 0], s_raw_l.at[h])
        sent(to_r.at[h], s_mix_r.at[h])
        sent(to_l.at[h], s_mix_l.at[h])
        sent(summed.at[h, 1:NZ], s_z.at[h])

    steps = tiles // STEP
    for d in (2, 6, 1, 7):
        pass_on(d)
    fill_panel(0)
    lax.fori_loop(0, steps // 2, forward(0), 0)
    for d in (3, 5):
        pass_on(d)
    lax.fori_loop(steps // 2, steps, forward(0), 0)
    pass_on(4)
    sums_start(0)
    fill_panel(1)
    lax.fori_loop(0, steps * 3 // 8, forward(1), 0)
    sums_relay(0, (0,))
    lax.fori_loop(steps * 3 // 8, steps * 5 // 8, forward(1), 0)
    sums_relay(0, (2,))
    lax.fori_loop(steps * 5 // 8, steps, forward(1), 0)
    sums_start(1)
    first = sums_z(0)
    sums_relay(1)
    second = sums_z(1)
    total = jnp.concatenate([sums_end(0, first), sums_end(1, second)], axis=0)

    ut = total.astype(BF16)
    un = total.T
    un_high = un.astype(BF16)
    un_low = (un - un_high.astype(F32)).astype(BF16)
    pre = jnp.dot(un_high, w_turned[...], preferred_element_type=F32) + bias_ref[...]
    pre = pre + jnp.dot(un_low, w_turned[...], preferred_element_type=F32)
    s = jax.nn.sigmoid(pre)
    grad = (cot_ref[...] * s * (1.0 + pre * (1.0 - s))).astype(BF16)
    own[...] = grad

    for d in near:
        go(own, band_ref.at[x, z], s_gz, r_gz.at[d], zdev(d))
    go(own, band_ref.at[x, z], s_gr, r_gl.at[0], xdev(right))
    go(own, band_ref.at[x, z], s_gl, r_gr.at[0], xdev(left))
    band_ref[x, z] = grad
    act_v[...] = pre * s
    act_out = pltpu.make_async_copy(act_v, act_ref, s_out.at[0])
    act_out.start()

    gw = jnp.dot(ut, grad, preferred_element_type=F32)
    for n, d in enumerate(PARTS[0] + PARTS[1]):
        for kk in range(NK):
            slot = ysource(d) * NK + kk
            at = (n * NK + kk) * 8
            wbuf[slot // NZ, slot % NZ] = gw[at : at + 8]
    gb = jnp.sum(grad.astype(F32), axis=0, keepdims=True)
    wbuf[2] = jnp.broadcast_to(gb.reshape(1, 1, T), (NZ, 8, T))
    wbuf[3] = jnp.zeros((NZ, 8, T), F32)

    half_a = (0, 7, 6, 5)

    def spread(d):
        zz = zfrom(d)
        arrived(band_ref.at[x, zz], s_gz, r_gz.at[d])
        go(band_ref.at[x, zz], band_ref.at[x, zz], s_gr, r_gl.at[d], xdev(right))
        go(band_ref.at[x, zz], band_ref.at[x, zz], s_gl, r_gr.at[d], xdev(left))

    def relay(d):
        zz = zfrom(d)
        arrived(band_ref.at[left, zz], s_gr, r_gl.at[d])
        if d in half_a:
            go(band_ref.at[left, zz], band_ref.at[left, zz], s_rel, r_rel.at[d], xdev(right))
        arrived(band_ref.at[right, zz], s_gr, r_gr.at[d])
        if d not in half_a:
            go(band_ref.at[right, zz], band_ref.at[right, zz], s_rel, r_rel.at[d], xdev(left))

    sent(ftraw.at[0 : NY - 1], s_fy)
    sent(ftraw.at[0:NY], s_fp)
    sums_sent(0)
    sums_sent(1)
    for d in (1, 7, 2, 6):
        spread(d)
    relay(0)
    spread(3)
    relay(1)
    spread(5)
    relay(7)
    spread(4)
    for d in far:
        go(wbuf.at[:, zof(d)], wzin.at[d], s_wz, r_wz.at[d], zdev(d))
    for d in (2, 6, 3, 5, 4):
        relay(d)
    wsum = wbuf[:, z]
    for d in near:
        arrived(wzin.at[d], s_wz, r_wz.at[d])
        wsum = wsum + wzin[d]
    wx[...] = wsum
    for e in (2, 1, 3):
        xx = lax.rem(x + e, NX)
        go(wx.at[xx], wxin.at[e], s_wx, r_wx.at[e], xdev(xx))
    for d in (0,) + near:
        arrived(band_ref.at[across, zfrom(d)], s_rel, r_rel.at[d])

    def backward(g, carry):
        for u in range(STEP):
            t = g * STEP + u
            r = rows_ref[0, t]
            prod = jnp.dot(dense[t], band_ref[r // NZ, r % NZ], preferred_element_type=F32)
            prefix[t] = prefix[table[2, t]] + prod
        return carry

    lax.fori_loop(0, steps // 8, backward, 0)
    wtotal = wx[x]
    for e in (1, 3, 2):
        arrived(wxin.at[e], s_wx, r_wx.at[e])
        wtotal = wtotal + wxin[e]
    wcol[...] = wtotal
    go(wcol, wpin, s_wp, r_wp, partner)
    lax.fori_loop(steps // 8, steps * 3 // 8, backward, 0)
    arrived(wpin, s_wp, r_wp)
    wpair = wtotal + wpin[...]
    wp[...] = wpair
    for d in far:
        go(wp, wyin.at[d], s_wy, r_wy.at[d], ydev(d))
    lax.fori_loop(steps * 3 // 8, steps, backward, 0)

    contract = (((1,), (1,)), ((), ()))
    for c in range(fbuf.shape[3] // T):
        value = prefix[table[3, c]]
        high = value.astype(BF16)
        low = (value - high.astype(F32)).astype(BF16)
        term = lax.dot_general(w_ref[...], high, contract, preferred_element_type=F32)
        term += lax.dot_general(w_ref[...], low, contract, preferred_element_type=F32)
        fbuf[:, :, :, c * T : (c + 1) * T] = term.reshape(NY, NK, 8, T)

    for d in far + (0,):
        go(fbuf.at[yof(d), 1 - k], pin.at[d], s_p, r_p.at[d], partner)
    wtotal = wpair
    for d in near:
        arrived(wyin.at[d], s_wy, r_wy.at[d])
        wtotal = wtotal + wyin[d]
    wt[...] = wtotal
    wall[x, z] = wtotal
    for d in far:
        arrived(pin.at[d], s_p, r_p.at[d])
        sbuf[d] = (pin[d] + fbuf[yof(d), k]).astype(BF16)
        go(sbuf.at[d], yin.at[d], s_y, r_y.at[d], ydev(d))
        if d == 4:
            for dz in far:
                go(wt, wall.at[x, z], s_oz, r_oz.at[dz], zdev(dz))
    arrived(pin.at[0], s_p, r_p.at[0])
    total = pin[0] + fbuf[y, k]
    sent(band_ref.at[0, 0 : NZ - 1], s_gz)
    for sem in (s_gr, s_gl, s_rel):
        sent(band_ref.at[0], sem)
    sent(wzin.at[1:NZ], s_wz)
    sent(wxin.at[1:NX], s_wx)
    sent(wpin, s_wp)
    sent(wyin.at[1:NY], s_wy)
    act_out.wait()
    for d in near:
        arrived(wall.at[x, zfrom(d)], s_oz, r_oz.at[d])
    for e in (2, 1, 3):
        go(wall.at[x], wall.at[x], s_ox, r_ox.at[e], xdev(lax.rem(x + e, NX)))
    for d in near:
        arrived(yin.at[d], s_y, r_y.at[d])
        total = total + yin[d].astype(F32)
    grad_v[...] = total.astype(BF16)
    grad_out = pltpu.make_async_copy(grad_v, grad_ref, s_out.at[1])
    grad_out.start()
    for e in (1, 3, 2):
        arrived(wall.at[lax.rem(x + NX - e, NX)], s_ox, r_ox.at[e])
    wall_out = pltpu.make_async_copy(wall, wout_ref, s_out.at[2])
    wall_out.start()
    sent(pin, s_p)
    sent(yin.at[1:NY], s_y)
    sent(wyin.at[1:NZ], s_oz)
    sent(wall.at[1:NX], s_ox)
    grad_out.wait()
    wall_out.wait()


def finish_kernel(shrink, act_ref, grad_ref, w_ref, act_out, grad_out, w_out, b_out):
    act_out[...] = act_ref[...]
    grad_out[...] = grad_ref[...]
    w_out[...] = w_ref[0:16].reshape(16 * 8, T) * shrink
    b_out[...] = w_ref[16][0:1, :] * shrink


def dma(*shape):
    return pltpu.SemaphoreType.DMA(shape)


def shards(features, weight, bias_vector, tile_rows, tile_cols, neighbours, edge_weights, tile_count, cotangent):
    nodes, width = features.shape
    hidden = weight.shape[1]
    tiles = neighbours.shape[2]
    shape = jax.ShapeDtypeStruct
    vbf = lambda *dims: pltpu.VMEM(dims, BF16)
    vf = lambda *dims: pltpu.VMEM(dims, F32)

    act, grad_t, wall = pl.pallas_call(
        whole_kernel,
        out_shape=(shape((T, hidden), F32), shape((width, nodes), BF16), shape((NX, NZ, 8, hidden), F32)),
        in_specs=[HBM_SPEC] * 9,
        out_specs=(HBM_SPEC,) * 3,
        scratch_shapes=[
            pltpu.SMEM((1, tiles), jnp.int32), pltpu.SMEM((1, tiles), jnp.int32), pltpu.SMEM((1, 1), jnp.int32),
            pltpu.VMEM((1, tiles), jnp.int32), pltpu.VMEM((1, tiles), jnp.int32),
            pltpu.VMEM(neighbours.shape[2:], jnp.int32), vbf(*edge_weights.shape[2:]),
            vbf(*weight.shape), vf(1, hidden), vf(T, hidden), dma(11),
            vf(NY * NK, 8, hidden), vbf(T, hidden), vbf(tiles, T, T), vf(tiles + 1, T, T), pltpu.VMEM((8, tiles), jnp.int32), pltpu.SMEM((8, tiles), jnp.int32),
            vbf(NY * NK, width, nodes), vbf(2, nodes // T, HALF, T), vbf(2, NX, NZ, HALF, T), vbf(NX, NZ, T, T),
            vf(NY, NK, width, nodes),
            vbf(2, 4, HALF, T), vbf(2, 4, HALF, T), vbf(2, 4, HALF, T), vbf(2, 4, HALF, T),
            vbf(2, NZ, HALF, T), vbf(2, NZ, HALF, T), vbf(2, NZ, HALF, T), vbf(2, NZ, HALF, T), vbf(T, T),
            vf(T, hidden), vbf(width, nodes), vf(NX, NZ, 8, T), dma(3),
            vf(NX, NZ, 8, T), vf(NX, 8, T), vf(NX, 8, T), vf(NZ, NX, 8, T),
            vf(8, T), vf(8, T), vf(8, T), vf(NY, 8, T), vf(8, T),
            vf(NY, width, nodes), vbf(NY, width, nodes), vbf(NY, width, nodes),
            dma(), dma(), dma(NY), dma(), dma(NY),
            dma(2), dma(2), dma(2), dma(2), dma(2, 4), dma(2, 4), dma(2, NZ), dma(2, NZ),
            dma(2), dma(2, NZ), dma(), dma(NZ), dma(), dma(), dma(NZ), dma(NZ), dma(), dma(NZ),
            dma(), dma(NX), dma(), dma(NZ),
            dma(), dma(NY), dma(), dma(NY), dma(), dma(), dma(), dma(NY), dma(), dma(NZ), dma(), dma(NX),
        ],
        compiler_params=pltpu.CompilerParams(collective_id=0, has_side_effects=True),
        name="whole",
    )(
        tile_rows[0], tile_cols[0], tile_count, features.T,
        neighbours[0, 0], edge_weights[0, 0], weight, bias_vector.reshape(1, hidden), cotangent,
    )

    node_count = cotangent.shape[0] * lax.axis_size("row") * lax.axis_size("col")
    shrink = float(node_count) ** (-0.5)
    act, grad_t, wgrad, bgrad = pl.pallas_call(
        functools.partial(finish_kernel, shrink),
        out_shape=(
            shape((T, hidden), F32), shape((width, nodes), BF16), shape((T, hidden), F32), shape((1, hidden), F32),
        ),
        in_specs=[VMEM_SPEC] * 3,
        out_specs=(VMEM_SPEC,) * 4,
        name="finish",
    )(act, grad_t, wall.reshape(NX * NZ, 8, hidden))
    return act, grad_t.T, wgrad, bgrad.reshape(hidden)


def solution(mesh):
    in_specs = (
        P("col", "row"),
        P(),
        P(),
        P("row", "col", None),
        P("row", "col", None),
        P("row", "col", None, None, None),
        P("row", "col", None, None, None),
        P("row", "col"),
        P(("row", "col"), None),
    )
    out_specs = (P(("row", "col"), None), P("col", "row"), P(), P())
    return jax.shard_map(shards, mesh=mesh, in_specs=in_specs, out_specs=out_specs, check_vma=False)
```
